512 devices in a mesh: dp: 4 (over y_lo), fsdp: 32 (over x, z), head: 4 (over y_hi, core).
Axes of the slice: x: 4, y: 8 (y_hi: 2, y_lo: 4; y = y_hi * 4 + y_lo), z: 8, core: 2. Of those that a mesh axis runs over, the one named last changes fastest.
Arguments:
- queries: bfloat16 [4, 8192, 2048], P('dp', 'fsdp', 'head'), may hold values from -8 to 8
- key_rows: bfloat16 [4, 8192, 2048], P('dp', 'fsdp', 'head'), may hold values from -8 to 8
- value_rows: bfloat16 [4, 8192, 2048], P('dp', 'fsdp', 'head'), may hold values from -6 to 6
- out_weight: bfloat16 [2048, 2048], P('fsdp', 'head'), may hold values from -0.125 to 0.125
- sum_lists: int32 [4, 64, 16], P('dp', 'fsdp'), may hold values from 0 to 31, as said below
- out_grad: bfloat16 [4, 8192, 2048], P('dp', 'fsdp', 'head'), may hold values from -6 to 6
Outputs:
- projected: bfloat16 [4, 8192, 2048], P('dp', 'fsdp', 'head')
- query_grad: bfloat16 [4, 8192, 2048], P('dp', 'fsdp', 'head')
- key_grad: bfloat16 [4, 8192, 2048], P('dp', 'fsdp', 'head')
- value_grad: bfloat16 [4, 8192, 2048], P('dp', 'fsdp', 'head')
- weight_grad: float32 [2048, 2048], P('fsdp', 'head')
The draws below stay inside these ranges and needn't reach their ends.
Inputs may be any that keep to these rules, and one draw needn't show every extreme that they name: `sum_lists`: each row names 16 different strides.
All inputs are finite; a program needn't handle non-finite values.
Results may differ from the reference program's by a relative error of at most 0.028.
Values may be sent and summed in bfloat16 or wider, within the bound.
A program may use at most 64 MiB of HBM per device.

```python
import math
import jax
import jax.numpy as jnp
from jax import lax

HS = 128
HEADS = 16
DOUT = 2048
BLK = 128
WIN = 3
STRIDE = 256
SUMC = 8
HW = 2048
SEQS = 4
L = 8192
NQB = 64
NSUM = 32
SEL = 16


def paired_rows(key):
    base_key = jax.random.fold_in(key, 4242)
    key_query, key_other = jax.random.split(base_key, 2)
    full_shape = (SEQS, L, HEADS * HS)
    query_out = jnp.clip(1.3 * jax.random.normal(key_query, full_shape, jnp.float32), -7.8, 7.8)
    key_out = jnp.clip(1.3 * jax.random.normal(key_other, full_shape, jnp.float32), -7.8, 7.8)
    return (query_out, key_out)


def draw_queries(key, part):
    return paired_rows(key)[0].astype(jnp.bfloat16)


def draw_key_rows(key, part):
    return paired_rows(key)[1].astype(jnp.bfloat16)


def draw_sum_lists(key, part):
    base_key = jax.random.fold_in(key, 77)
    row_keys = jax.random.split(base_key, SEQS * NQB)
    chosen = jax.vmap(lambda row_key: jax.random.permutation(row_key, NSUM)[:SEL])(row_keys)
    return chosen.reshape(SEQS, NQB, SEL).astype(jnp.int32)


def shard_levels(rng, dims, cuts, smallest, high):
    loudness = 1.0
    for axis_at, shards_of in cuts:
        draws = jax.random.uniform(jax.random.fold_in(jax.random.fold_in(rng, 6), axis_at), (shards_of,), jnp.float32, smallest / len(cuts), high / len(cuts))
        loudness = loudness * jnp.repeat(jnp.exp(draws), dims[axis_at] // shards_of).reshape((-1,) + (1,) * (len(dims) - 1 - axis_at))
    return loudness


def bell_draw(stream_key, shape, width, most, cuts=(), held_as=jnp.bfloat16):
    loudness = shard_levels(stream_key, shape, cuts, -0.22, 0.18) if cuts else 1.0
    values = jax.random.normal(stream_key, shape, jnp.float32) * width * loudness
    return jnp.minimum(jnp.maximum(values, -most), most).astype(held_as)


def setup_inputs(seed: int = 0) -> dict:
    streams_of = jax.random.split(jax.random.key(seed), 7)
    return {
        "queries": draw_queries(jax.random.fold_in(streams_of[6], 71), 0),
        "key_rows": draw_key_rows(jax.random.fold_in(streams_of[6], 71), 0),
        "value_rows": bell_draw(streams_of[2], (SEQS, L, HW), 1.0, 6.0, ((0, 4), (1, 32), (2, 4))),
        "out_weight": bell_draw(streams_of[3], (HW, DOUT), HW ** -0.5, 0.125, ((0, 32), (1, 4))),
        "sum_lists": draw_sum_lists(jax.random.fold_in(streams_of[6], 71), 0),
        "out_grad": bell_draw(streams_of[5], (SEQS, L, DOUT), 1.0, 6.0, ((0, 4), (1, 32), (2, 4))),
    }


def softmax_rows(scores, allowed):
    scores = jnp.where(allowed[None], scores, -jnp.inf)
    peak = lax.optimization_barrier(jnp.max(scores, axis=2, keepdims=True))
    raised = jnp.exp(scores - peak)
    return raised / lax.optimization_barrier(jnp.sum(raised, axis=2, keepdims=True))

def block_allowed(block_id, chosen):
    query_pos = block_id * BLK + jnp.arange(BLK, dtype=jnp.int32)
    window_start = (block_id - WIN + 1) * BLK
    key_pos = window_start + jnp.arange(WIN * BLK, dtype=jnp.int32)
    nearby = (key_pos[None, :] >= 0) & (key_pos[None, :] <= query_pos[:, None])
    distant = (chosen + 1) * STRIDE <= window_start
    distant = jnp.broadcast_to(jnp.repeat(distant, SUMC)[None, :], (BLK, SEL * SUMC))
    return jnp.concatenate([nearby, distant], axis=1)

def block_rows(padded, summary, block_id, chosen):
    nearby = lax.dynamic_slice_in_dim(padded, (block_id * BLK).astype(jnp.int32), WIN * BLK, 0)
    distant = summary[chosen].reshape(SEL * SUMC, HEADS, HS)
    return jnp.concatenate([nearby, distant], axis=0)

def bf16_round(entries):
    return lax.optimization_barrier(entries.astype(jnp.bfloat16)).astype(jnp.float32)

def add_window(total, addend, start_row):
    current = lax.dynamic_slice_in_dim(total, start_row, WIN * BLK, 0)
    return lax.dynamic_update_slice_in_dim(total, current + addend, start_row, 0)

def sequence_pass(query_seq, key_seq, value_seq, chosen_seq, grad_seq, out_weight):
    score_scale = 1.0 / math.sqrt(HS)
    query_f = query_seq.astype(jnp.float32).reshape(L, HEADS, HS)
    key_f = key_seq.astype(jnp.float32).reshape(L, HEADS, HS)
    value_f = value_seq.astype(jnp.float32).reshape(L, HEADS, HS)
    leading = jnp.zeros(((WIN - 1) * BLK, HEADS, HS), jnp.float32)
    key_pad = jnp.concatenate([leading, key_f], axis=0)
    value_pad = jnp.concatenate([leading, value_f], axis=0)
    key_far = key_f.reshape(NSUM, STRIDE, HEADS, HS)[:, STRIDE - SUMC:]
    value_far = value_f.reshape(NSUM, STRIDE, HEADS, HS)[:, STRIDE - SUMC:]
    block_list = jnp.arange(NQB, dtype=jnp.int32)

    def block_weights(block_id):
        chosen = chosen_seq[block_id]
        query_blk = lax.dynamic_slice_in_dim(query_f, (block_id * BLK).astype(jnp.int32), BLK, 0)
        key_blk = block_rows(key_pad, key_far, block_id, chosen)
        value_blk = block_rows(value_pad, value_far, block_id, chosen)
        scores = jnp.einsum('ihd,jhd->hij', query_blk, key_blk) * score_scale
        weights = softmax_rows(scores, block_allowed(block_id, chosen))
        return (chosen, query_blk, key_blk, value_blk, weights)

    def attend(block_id):
        chosen, query_blk, key_blk, value_blk, weights = block_weights(block_id)
        return jnp.einsum('hij,jhd->ihd', bf16_round(weights), value_blk).astype(jnp.bfloat16)
    mixed = lax.map(attend, block_list).reshape(L, HEADS * HS)
    projected = jnp.dot(mixed, out_weight, preferred_element_type=jnp.float32).astype(jnp.bfloat16)
    grad_mixed = jnp.dot(grad_seq, out_weight.T, preferred_element_type=jnp.float32).astype(jnp.bfloat16)
    weight_part = jnp.dot(mixed.T, grad_seq, preferred_element_type=jnp.float32)
    mixed_f = mixed.astype(jnp.float32).reshape(L, HEADS, HS)
    grad_f = grad_mixed.astype(jnp.float32).reshape(L, HEADS, HS)

    def backward(totals, block_id):
        key_acc, value_acc, key_far_acc, value_far_acc = totals
        chosen, query_blk, key_blk, value_blk, weights = block_weights(block_id)
        weights_b = bf16_round(weights)
        start_row = (block_id * BLK).astype(jnp.int32)
        grad_blk = lax.dynamic_slice_in_dim(grad_f, start_row, BLK, 0)
        mixed_blk = lax.dynamic_slice_in_dim(mixed_f, start_row, BLK, 0)
        delta = lax.optimization_barrier(jnp.sum(grad_blk * mixed_blk, axis=2))
        dprob = jnp.einsum('ihd,jhd->hij', grad_blk, value_blk)
        dscore = bf16_round(weights * (dprob - delta.T[:, :, None]))
        query_part = (jnp.einsum('hij,jhd->ihd', dscore, key_blk) * score_scale).astype(jnp.bfloat16)
        key_part = jnp.einsum('hij,ihd->jhd', dscore, query_blk) * score_scale
        value_part = jnp.einsum('hij,ihd->jhd', weights_b, grad_blk)
        key_acc = add_window(key_acc, key_part[:WIN * BLK], start_row)
        value_acc = add_window(value_acc, value_part[:WIN * BLK], start_row)
        key_far_acc = key_far_acc.at[chosen].add(key_part[WIN * BLK:].reshape(SEL, SUMC, HEADS, HS))
        value_far_acc = value_far_acc.at[chosen].add(value_part[WIN * BLK:].reshape(SEL, SUMC, HEADS, HS))
        return ((key_acc, value_acc, key_far_acc, value_far_acc), query_part)
    zero_pad = jnp.zeros(((WIN - 1) * BLK + L, HEADS, HS), jnp.float32)
    zero_far = jnp.zeros((NSUM, SUMC, HEADS, HS), jnp.float32)
    totals, query_grad = lax.scan(backward, (zero_pad, zero_pad, zero_far, zero_far), block_list)

    def finish(accum, far_accum):
        own_rows = accum[(WIN - 1) * BLK:].reshape(NSUM, STRIDE, HEADS, HS)
        own_rows = own_rows.at[:, STRIDE - SUMC:].add(far_accum)
        return own_rows.reshape(L, HEADS * HS).astype(jnp.bfloat16)
    key_grad = finish(totals[0], totals[2])
    value_grad = finish(totals[1], totals[3])
    return (projected, query_grad.reshape(L, HEADS * HS), key_grad, value_grad, weight_part)

def reference(queries, key_rows, value_rows, out_weight, sum_lists, out_grad):

    def one_sequence(operands):
        query_seq, key_seq, value_seq, chosen_seq, grad_seq = operands
        return sequence_pass(query_seq, key_seq, value_seq, chosen_seq, grad_seq, out_weight)
    projected, query_grad, key_grad, value_grad, weight_parts = lax.map(one_sequence, (queries, key_rows, value_rows, sum_lists, out_grad))
    return (projected, query_grad, key_grad, value_grad, lax.optimization_barrier(jnp.sum(weight_parts, axis=0)))
```

```python
import math

import jax
import jax.numpy as jnp
from jax import lax
from jax.experimental import pallas as pl
from jax.experimental.pallas import tpu as pltpu
from jax.sharding import PartitionSpec as P

HS = 128
BLK = 128
STRIDE = 256
SUMC = 8
NX = 4
NZ = 8
NH = 4
ND = 4
TOK = 256
WID = 512
ROWS = 64
HALF = ROWS // 2
HEADS = WID // HS
FSDP = NX * NZ
SCALE = 1.0 / math.sqrt(HS)
NEG = -1e30
MESH = pl.DeviceIdType.MESH
BF = jnp.bfloat16
F32 = jnp.float32


def place():
    d = lax.axis_index("dp")
    f = lax.axis_index("fsdp")
    h = lax.axis_index("head")
    return d, lax.div(f, NZ), lax.rem(f, NZ), h


def send(src, dst, ssem, rsem, dev):
    return pltpu.make_async_remote_copy(
        src_ref=src, dst_ref=dst, send_sem=ssem, recv_sem=rsem, device_id=dev, device_id_type=MESH
    )


def meet(bar, count, swapped):
    @pl.when(swapped)
    def _():
        pl.semaphore_wait(bar, count + 1)

    @pl.when(jnp.logical_not(swapped))
    def _():
        pl.semaphore_wait(bar, count)


class Links:
    def __init__(self):
        self.d, self.x, self.z, self.h = place()
        d, x, z, h = self.d, self.x, self.z, self.h
        self.xr, self.xl = lax.rem(x + 1, NX), lax.rem(x + NX - 1, NX)
        self.xo = lax.rem(x + 2, NX)
        self.zr, self.zl = lax.rem(z + 1, NZ), lax.rem(z + NZ - 1, NZ)
        f = x * NZ + z
        self.f = f
        self.sib = h + 1 - 2 * lax.rem(h, 2)
        self.rem = lax.rem(h + 2, NH)
        self.far = lax.rem(self.sib + 2, NH)
        self.dev_xr = (d, self.xr * NZ + z, h)
        self.dev_xl = (d, self.xl * NZ + z, h)
        self.dev_zr = (d, x * NZ + self.zr, h)
        self.dev_zl = (d, x * NZ + self.zl, h)
        self.dev_next = (d, lax.rem(f + 1, FSDP), h)
        self.dev_prev = (d, lax.rem(f + FSDP - 1, FSDP), h)
        self.dev_sib = (d, f, self.sib)
        self.dev_rem = (d, f, self.rem)
        self.dev_swap = (d, h * NZ + z, x)
        self.zs = [lax.rem(z + i, NZ) for i in range(NZ)]
        self.xs = [lax.rem(x + i, NX) for i in range(NX)]

    def dev_z(self, i):
        return (self.d, self.x * NZ + self.zs[i], self.h)

    def dev_x(self, i):
        return (self.d, self.xs[i] * NZ + self.z, self.h)


def gather_kernel(
    w_ref, g_ref, k_ref, v_ref, t_ref,
    wf, ga, pk, pv, sa,
    swap_sem, loc_sem, zr_s, zr_r, zl_s, zl_r, xr_s, xr_r, xl_s, xl_r, fr_s, fr_r, fl_s, fl_r,
    kv_s, kv_r, g_s, g_r, sz_s, sz_r, sx_s, sx_r,
):
    m = Links()
    d, x, z, h = m.d, m.x, m.z, m.h
    bar = pltpu.get_barrier_semaphore()

    def hello(dev):
        pl.semaphore_signal(bar, inc=1, device_id=dev, device_id_type=MESH)

    for i in range(1, NZ):
        hello(m.dev_z(i))
    for i in range(1, NX):
        hello(m.dev_x(i))
    hello(m.dev_sib)
    hello(m.dev_rem)
    hello(m.dev_next)
    hello(m.dev_prev)
    swapped = x != h

    @pl.when(swapped)
    def _():
        hello(m.dev_swap)

    meet(bar, (NZ - 1) + (NX - 1) + 4, swapped)

    @pl.when(swapped)
    def _():
        send(w_ref, wf.at[h, z], swap_sem.at[0], swap_sem.at[1], m.dev_swap).start()

    @pl.when(jnp.logical_not(swapped))
    def _():
        pltpu.make_async_copy(w_ref, wf.at[x, z], loc_sem.at[0]).start()

    own_t = pltpu.make_async_copy(t_ref, sa.at[x, z], loc_sem.at[1])
    own_t.start()
    tz = [send(t_ref, sa.at[x, z], sz_s.at[i - 1], sz_r.at[i - 1], m.dev_z(i)) for i in range(1, NZ)]
    for c in tz:
        c.start()
    own_g = pltpu.make_async_copy(g_ref, ga.at[h], loc_sem.at[2])
    own_g.start()
    g_rem = send(g_ref, ga.at[h], g_s.at[0], g_r.at[0], m.dev_rem)
    g_rem.start()
    g_sib = send(g_ref, ga.at[h], g_s.at[1], g_r.at[1], m.dev_sib)
    g_sib.start()
    ks = send(k_ref, pk, kv_s.at[0], kv_r.at[0], m.dev_next)
    ks.start()
    vs = send(v_ref, pv, kv_s.at[1], kv_r.at[1], m.dev_next)
    vs.start()

    @pl.when(swapped)
    def _():
        send(w_ref, wf.at[h, z], swap_sem.at[0], swap_sem.at[1], m.dev_swap).wait()

    @pl.when(jnp.logical_not(swapped))
    def _():
        pltpu.make_async_copy(w_ref, wf.at[x, z], loc_sem.at[0]).wait()

    pending = [own_t, own_g, g_sib]
    sends = list(tz) + [g_rem, ks, vs]

    order = [("own", 0), ("r", 1), ("l", 1), ("r", 2), ("l", 2), ("r", 3), ("l", 3), ("r", 4)]
    where = []
    for kind, s in order:
        where.append(z if kind == "own" else m.zs[(NZ - s) % NZ] if kind == "r" else m.zs[s])

    def zright(s):
        slot = wf.at[x, m.zs[(NZ - s) % NZ]]
        return send(slot, slot, zr_s.at[s], zr_r.at[s], m.dev_zr)

    def zleft(s):
        slot = wf.at[x, m.zs[s]]
        return send(slot, slot, zl_s.at[s], zl_r.at[s], m.dev_zl)

    def xsend(n):
        slot = wf.at[x, where[n]]
        return (
            send(slot, slot, xr_s.at[n], xr_r.at[n], m.dev_xr),
            send(slot, slot, xl_s.at[n], xl_r.at[n], m.dev_xl),
        )

    def xforward(n):
        a = wf.at[m.xl, where[n], pl.ds(0, HALF)]
        b = wf.at[m.xr, where[n], pl.ds(HALF, HALF)]
        return (
            send(a, a, fr_s.at[n], fr_r.at[n], m.dev_xr),
            send(b, b, fl_s.at[n], fl_r.at[n], m.dev_xl),
        )

    zrs = {}
    zls = {}
    xsd = {}
    xfd = {}

    def forward(n):
        xsd[n][0].wait_recv()
        xfd[n] = xforward(n)
        xfd[n][0].start()
        xsd[n][1].wait_recv()
        xfd[n][1].start()

    g_rem_pass = send(ga.at[m.rem], ga.at[m.rem], g_s.at[2], g_r.at[2], m.dev_sib)
    xsum = []
    for n, (kind, s) in enumerate(order):
        if kind == "own":
            zrs[0], zls[0] = zright(0), zleft(0)
            zrs[0].start()
            zls[0].start()
        elif kind == "r":
            zrs[s - 1].wait_recv()
            if s < 4:
                zrs[s] = zright(s)
                zrs[s].start()
        else:
            zls[s - 1].wait_recv()
            if s < 3:
                zls[s] = zleft(s)
                zls[s].start()
        xsd[n] = xsend(n)
        xsd[n][0].start()
        xsd[n][1].start()
        if n == 2:
            own_t.wait()
            for c in tz:
                c.wait_recv()
            slab = sa.at[x]
            for i in range(1, NX):
                c = send(slab, slab, sx_s.at[i - 1], sx_r.at[i - 1], m.dev_x(i))
                c.start()
                xsum.append(c)
        if n >= 2:
            forward(n - 2)
    forward(NZ - 2)
    g_rem.wait_recv()
    g_rem_pass.start()
    forward(NZ - 1)
    for n in range(NZ):
        xfd[n][0].wait_recv()
        xfd[n][1].wait_recv()
    own_g.wait()
    ks.wait_recv()
    vs.wait_recv()
    g_sib.wait_recv()
    g_rem_pass.wait_recv()
    for c in xsum:
        c.wait_recv()
    for c in tz + [g_rem, g_sib, g_rem_pass, ks, vs] + xsum:
        c.wait_send()
    for c in list(zrs.values()) + list(zls.values()):
        c.wait_send()
    for n in range(NZ):
        for c in (*xsd[n], *xfd[n]):
            c.wait_send()


def vmem(n):
    return [pl.BlockSpec(memory_space=pltpu.VMEM)] * n


def gather_inputs(w, g, k, v, t):
    dma = pltpu.SemaphoreType.DMA
    return pl.pallas_call(
        gather_kernel,
        name="gather_inputs",
        out_shape=(
            jax.ShapeDtypeStruct((NX, NZ, ROWS, WID), BF),
            jax.ShapeDtypeStruct((NH, TOK, WID), BF),
            jax.ShapeDtypeStruct((TOK, WID), BF),
            jax.ShapeDtypeStruct((TOK, WID), BF),
            jax.ShapeDtypeStruct((NX, NZ, 2, SUMC, WID), BF),
        ),
        in_specs=vmem(5),
        out_specs=tuple(vmem(5)),
        scratch_shapes=[dma((2,)), dma((3,))]
        + [dma((4,)), dma((4,)), dma((3,)), dma((3,))]
        + [dma((NZ,))] * 8
        + [dma((2,)), dma((2,)), dma((3,)), dma((3,))]
        + [dma((NZ - 1,)), dma((NZ - 1,)), dma((NX - 1,)), dma((NX - 1,))],
        compiler_params=pltpu.CompilerParams(
            collective_id=0, has_side_effects=True, vmem_limit_bytes=20 << 20
        ),
    )(w, g, k, v, t)


def dot_nt(a, b):
    return lax.dot_general(a, b, (((1,), (1,)), ((), ())), preferred_element_type=F32)


def dot_tn(a, b):
    return lax.dot_general(a, b, (((0,), (0,)), ((), ())), preferred_element_type=F32)


def dot_nn(a, b):
    return lax.dot_general(a, b, (((1,), (0,)), ((), ())), preferred_element_type=F32)


def attend_kernel(
    q_ref, k_ref, v_ref, pk, pv, sa, wf, ga, bias_ref,
    pp, pw, dq, dko, dvo, dkb, dvb, ds,
    gm_s, mx_s, sk_s, sv_s,
):
    first = lax.axis_index("fsdp") == 0
    sk_s[...] = sa[:, :, 0].astype(F32).reshape(TOK, WID).astype(BF)
    sv_s[...] = sa[:, :, 1].astype(F32).reshape(TOK, WID).astype(BF)
    gm = dot_nt(ga[0], wf[0].reshape(WID, WID))
    for c in range(1, NX):
        gm += dot_nt(ga[c], wf[c].reshape(WID, WID))
    gm_s[...] = gm.astype(BF)
    key_at = lax.broadcasted_iota(jnp.int32, (TOK, TOK), 0)
    query_at = lax.broadcasted_iota(jnp.int32, (TOK, TOK), 1)
    own_bias = jnp.where(key_at <= query_at, 0.0, NEG)
    low = jnp.where(query_at < BLK, 0, BLK) + jnp.where(first, 2 * TOK, 0)
    prior_bias = jnp.where(key_at >= low, 0.0, NEG)
    far_bias = bias_ref[...]
    for n in range(HEADS):
        cols = pl.ds(n * HS, HS)
        q = q_ref[:, cols]
        keys = (pk[:, cols], k_ref[:, cols], sk_s[:, cols])
        values = (pv[:, cols], v_ref[:, cols], sv_s[:, cols])
        scores = [
            dot_nt(key, q) * SCALE + bias
            for key, bias in zip(keys, (prior_bias, own_bias, far_bias))
        ]
        peak = jnp.max(jnp.maximum(jnp.maximum(scores[0], scores[1]), scores[2]), axis=0, keepdims=True)
        raised = [jnp.exp(s - peak) for s in scores]
        total = jnp.sum(raised[0] + raised[1] + raised[2], axis=0, keepdims=True)
        scale = 1.0 / total
        weights = [e * scale for e in raised]
        weights_b = [e.astype(BF) for e in weights]
        mixed_t = dot_tn(values[0], weights_b[0])
        for value, e in zip(values[1:], weights_b[1:]):
            mixed_t += dot_tn(value, e)
        mixed_tb = mixed_t.astype(BF)
        mx_s[:, cols] = mixed_t.T.astype(BF)
        for c in range(NH):
            part = dot_nn(mixed_tb, ga[c]).astype(BF)
            pw[c, pl.ds(2 * n, 2)] = part.reshape(2, ROWS, WID)
        grad = gm_s[:, cols]
        delta = jnp.sum(grad.astype(F32).T * mixed_tb.astype(F32), axis=0, keepdims=True)
        dscore = [
            (e * (dot_nt(value, grad) - delta)).astype(BF) for e, value in zip(weights, values)
        ]
        dq_t = dot_tn(keys[0], dscore[0])
        for key, e in zip(keys[1:], dscore[1:]):
            dq_t += dot_tn(key, e)
        dq[:, cols] = (dq_t.T * SCALE).astype(BF)
        dkb[:, cols] = (dot_nn(dscore[0], q) * SCALE).astype(BF)
        dko[:, cols] = dot_nn(dscore[1], q) * SCALE
        far_k = dot_nn(dscore[2], q) * SCALE
        ds[:, :, 0, :, cols] = far_k.reshape(NX, NZ, SUMC, HS).astype(BF)
        dvb[:, cols] = dot_nn(weights_b[0], grad).astype(BF)
        dvo[:, cols] = dot_nn(weights_b[1], grad)
        far_v = dot_nn(weights_b[2], grad)
        ds[:, :, 1, :, cols] = far_v.reshape(NX, NZ, SUMC, HS).astype(BF)
    for c in range(NH):
        pp[c] = dot_nn(mx_s[...], wf[c].reshape(WID, WID)).astype(BF)


def attend(q, k, v, pk, pv, sa, wf, ga, bias):
    return pl.pallas_call(
        attend_kernel,
        name="attend",
        out_shape=(
            jax.ShapeDtypeStruct((NH, TOK, WID), BF),
            jax.ShapeDtypeStruct((NH, NZ, ROWS, WID), BF),
            jax.ShapeDtypeStruct((TOK, WID), BF),
            jax.ShapeDtypeStruct((TOK, WID), F32),
            jax.ShapeDtypeStruct((TOK, WID), F32),
            jax.ShapeDtypeStruct((TOK, WID), BF),
            jax.ShapeDtypeStruct((TOK, WID), BF),
            jax.ShapeDtypeStruct((NX, NZ, 2, SUMC, WID), BF),
        ),
        in_specs=vmem(9),
        out_specs=tuple(vmem(8)),
        scratch_shapes=[pltpu.VMEM((TOK, WID), BF)] * 4,
        compiler_params=pltpu.CompilerParams(vmem_limit_bytes=30 << 20),
    )(q, k, v, pk, pv, sa, wf, ga, bias)


def reduce_kernel(
    pp, pw, dko, dvo, dkb, dvb, ds,
    proj, kg, vg, wg,
    arm, xrm, back, pin, bx, zin, zout, fin, fout, sx, szo, szi,
    a_s, a_r, b_s, b_r, z_s, z_r, f_s, f_r, loc_sem, bk_s, bk_r, p_s, p_r, sx_s, sx_r, sz_s, sz_r,
):
    m = Links()
    d, x, z, h = m.d, m.x, m.z, m.h
    bar = pltpu.get_barrier_semaphore()

    def hello(dev):
        pl.semaphore_signal(bar, inc=1, device_id=dev, device_id_type=MESH)

    def owner(i):
        return (lax.rem(d + i, ND), h * NZ + z, x)

    for i in range(1, NZ):
        hello(m.dev_z(i))
    for i in range(1, NX):
        hello(m.dev_x(i))
    hello(m.dev_sib)
    hello(m.dev_rem)
    hello(m.dev_next)
    hello(m.dev_prev)
    for i in range(1, ND):
        hello(owner(i))
    swapped = x != h

    @pl.when(swapped)
    def _():
        hello(owner(0))

    meet(bar, (NZ - 1) + (NX - 1) + 4 + (ND - 1), swapped)

    rows = [m.zs[(i + 1) % NZ] for i in range(NZ)]

    def leg_a(n):
        r = rows[n]
        return (
            send(pw.at[m.xo, r, pl.ds(0, HALF)], arm.at[0, n], a_s.at[0, n], a_r.at[0, n], m.dev_xr),
            send(pw.at[m.xo, r, pl.ds(HALF, HALF)], arm.at[1, n], a_s.at[1, n], a_r.at[1, n], m.dev_xl),
        )

    a_legs = [leg_a(n) for n in range(NZ)]
    for n in range(NZ):
        a_legs[n][0].start()
        a_legs[n][1].start()
    s_legs = [
        send(ds.at[m.xs[i]], sx.at[i - 1], sx_s.at[i - 1], sx_r.at[i - 1], m.dev_x(i)) for i in range(1, NX)
    ]
    for c in s_legs:
        c.start()
    bk = (
        send(dkb, back.at[0], bk_s.at[0], bk_r.at[0], m.dev_prev),
        send(dvb, back.at[1], bk_s.at[1], bk_r.at[1], m.dev_prev),
    )
    p_legs = [
        send(pp.at[m.far], pin.at[0], p_s.at[0], p_r.at[0], m.dev_sib),
        send(pp.at[m.sib], pin.at[1], p_s.at[1], p_r.at[1], m.dev_sib),
    ]
    p_legs[0].start()
    p_legs[1].start()
    bk[0].start()
    bk[1].start()
    p_legs[0].wait_recv()
    pin[3] = (pin[0].astype(F32) + pp[m.rem].astype(F32)).astype(BF)

    def leg_b(n):
        return (
            send(bx.at[0, n], xrm.at[0, n], b_s.at[0, n], b_r.at[0, n], m.dev_xr),
            send(bx.at[1, n], xrm.at[1, n], b_s.at[1, n], b_r.at[1, n], m.dev_xl),
        )

    b_legs = {}
    z_legs = {}

    def stage_b(n):
        r = rows[n]
        a_legs[n][0].wait_recv()
        bx[0, n, pl.ds(0, HALF)] = (
            arm[0, n].astype(F32) + pw[m.xr, r, pl.ds(0, HALF)].astype(F32)
        ).astype(BF)
        bx[0, n, pl.ds(HALF, HALF)] = pw[m.xr, r, pl.ds(HALF, HALF)]
        a_legs[n][1].wait_recv()
        bx[1, n, pl.ds(0, HALF)] = pw[m.xl, r, pl.ds(0, HALF)]
        bx[1, n, pl.ds(HALF, HALF)] = (
            arm[1, n].astype(F32) + pw[m.xl, r, pl.ds(HALF, HALF)].astype(F32)
        ).astype(BF)
        b_legs[n] = leg_b(n)
        b_legs[n][0].start()
        b_legs[n][1].start()

    def stage_z(n):
        b_legs[n][0].wait_recv()
        b_legs[n][1].wait_recv()
        zout[n] = (
            xrm[0, n].astype(F32) + xrm[1, n].astype(F32) + pw[x, rows[n]].astype(F32)
        ).astype(BF)
        if n < NZ - 1:
            z_legs[n] = send(zout.at[n], zin.at[n], z_s.at[n], z_r.at[n], m.dev_z(n + 1))
            z_legs[n].start()

    stage_b(0)
    p_legs.append(send(pin.at[3], pin.at[2], p_s.at[2], p_r.at[2], m.dev_rem))
    p_legs[2].start()
    stage_b(1)
    for c in s_legs:
        c.wait_recv()
    szo[...] = (
        (ds[x].astype(F32) + sx[0].astype(F32)) + (sx[1].astype(F32) + sx[2].astype(F32))
    ).astype(BF)
    t_legs = [
        send(szo.at[m.zs[i]], szi.at[i - 1], sz_s.at[i - 1], sz_r.at[i - 1], m.dev_z(i)) for i in range(1, NZ)
    ]
    for c in t_legs:
        c.start()
    for n in range(2, NZ):
        stage_b(n)
        stage_z(n - 2)
    stage_z(NZ - 2)
    stage_z(NZ - 1)
    total = zout[NZ - 1].astype(F32)
    for n in range(NZ - 1):
        z_legs[n].wait_recv()
        total += zin[n].astype(F32)
    fout[...] = total.astype(BF)
    f_legs = [send(fout, fin.at[i], f_s.at[i], f_r.at[i], owner(i)) for i in range(ND)]
    for i in range(1, ND):
        f_legs[i].start()

    @pl.when(swapped)
    def _():
        f_legs[0].start()

    @pl.when(jnp.logical_not(swapped))
    def _():
        pltpu.make_async_copy(fout, fin.at[0], loc_sem).start()

    p_legs[1].wait_recv()
    p_legs[2].wait_recv()
    proj[...] = (pp[h].astype(F32) + pin[1].astype(F32) + pin[2].astype(F32)).astype(BF)
    own = szo[z].astype(F32)
    for i in range(NZ - 1):
        t_legs[i].wait_recv()
        own += szi[i].astype(F32)
    keep = jnp.where(m.f == FSDP - 1, 0.0, 1.0)
    for j, (out, mine) in enumerate(((kg, dko), (vg, dvo))):
        bk[j].wait_recv()
        out[pl.ds(0, TOK - 16)] = (
            mine[pl.ds(0, TOK - 16)] + back[j, pl.ds(0, TOK - 16)].astype(F32) * keep
        ).astype(BF)
        tail = mine[pl.ds(TOK - 16, 16)] + back[j, pl.ds(TOK - 16, 16)].astype(F32) * keep
        tail += jnp.concatenate([jnp.zeros((8, WID), F32), own[j]], axis=0)
        out[pl.ds(TOK - 16, 16)] = tail.astype(BF)

    for i in range(1, ND):
        f_legs[i].wait_recv()

    @pl.when(swapped)
    def _():
        f_legs[0].wait()

    @pl.when(jnp.logical_not(swapped))
    def _():
        pltpu.make_async_copy(fout, fin.at[0], loc_sem).wait()

    wg[...] = (fin[0].astype(F32) + fin[1].astype(F32)) + (fin[2].astype(F32) + fin[3].astype(F32))
    for c in s_legs + list(bk) + p_legs + t_legs + f_legs[1:]:
        c.wait_send()
    for n in range(NZ):
        for c in (*a_legs[n], *b_legs[n]):
            c.wait_send()
    for c in z_legs.values():
        c.wait_send()


def reduce_gradients(pp, pw, dko, dvo, dkb, dvb, ds):
    dma = pltpu.SemaphoreType.DMA
    return pl.pallas_call(
        reduce_kernel,
        name="reduce_gradients",
        out_shape=(
            jax.ShapeDtypeStruct((TOK, WID), BF),
            jax.ShapeDtypeStruct((TOK, WID), BF),
            jax.ShapeDtypeStruct((TOK, WID), BF),
            jax.ShapeDtypeStruct((ROWS, WID), F32),
        ),
        in_specs=vmem(7),
        out_specs=tuple(vmem(4)),
        scratch_shapes=[
            pltpu.VMEM((2, NZ, HALF, WID), BF),
            pltpu.VMEM((2, NZ, ROWS, WID), BF),
            pltpu.VMEM((2, TOK, WID), BF),
            pltpu.VMEM((4, TOK, WID), BF),
            pltpu.VMEM((2, NZ, ROWS, WID), BF),
            pltpu.VMEM((NZ - 1, ROWS, WID), BF),
            pltpu.VMEM((NZ, ROWS, WID), BF),
            pltpu.VMEM((ND, ROWS, WID), BF),
            pltpu.VMEM((ROWS, WID), BF),
            pltpu.VMEM((NX - 1, NZ, 2, SUMC, WID), BF),
            pltpu.VMEM((NZ, 2, SUMC, WID), BF),
            pltpu.VMEM((NZ - 1, 2, SUMC, WID), BF),
        ]
        + [dma((2, NZ))] * 4
        + [dma((NZ - 1,)), dma((NZ - 1,)), dma((ND,)), dma((ND,)), dma]
        + [dma((2,)), dma((2,)), dma((3,)), dma((3,))]
        + [dma((NX - 1,)), dma((NX - 1,)), dma((NZ - 1,)), dma((NZ - 1,))],
        compiler_params=pltpu.CompilerParams(
            collective_id=1, has_side_effects=True, vmem_limit_bytes=30 << 20
        ),
    )(pp, pw, dko, dvo, dkb, dvb, ds)


def body(queries, key_rows, value_rows, out_weight, sum_lists, out_grad):
    q, k, v, g = queries[0], key_rows[0], value_rows[0], out_grad[0]
    tails = jnp.stack([k[TOK - SUMC :], v[TOK - SUMC :]])
    strides = jnp.arange(FSDP, dtype=jnp.int32)
    block = lax.axis_index("fsdp") * 2 + jnp.arange(2, dtype=jnp.int32)
    named = jnp.any(sum_lists[0][:, :, None] == strides[None, None, :], axis=1)
    usable = named & ((strides[None, :] + 1) * STRIDE <= (block[:, None] - 2) * BLK)
    bias = jnp.where(usable, 0.0, NEG).astype(F32)
    bias = jnp.broadcast_to(bias.T[:, None, :, None], (FSDP, SUMC, 2, BLK)).reshape(TOK, TOK)
    wf, ga, pk, pv, sa = gather_inputs(out_weight, g, k, v, tails)
    pp, pw, dq, dko, dvo, dkb, dvb, ds = attend(q, k, v, pk, pv, sa, wf, ga, bias)
    proj, kg, vg, wg = reduce_gradients(pp, pw, dko, dvo, dkb, dvb, ds)
    return proj[None], dq[None], kg[None], vg[None], wg


def solution(mesh):
    tokens = P("dp", "fsdp", "head")
    return jax.shard_map(
        body,
        mesh=mesh,
        in_specs=(tokens, tokens, tokens, P("fsdp", "head"), P("dp", "fsdp", None), tokens),
        out_specs=(tokens, tokens, tokens, tokens, P("fsdp", "head")),
        check_vma=False,
    )
```

```python
import math

import jax
import jax.numpy as jnp
from jax import lax
from jax.experimental import pallas as pl
from jax.experimental.pallas import tpu as pltpu
from jax.sharding import PartitionSpec as P

HS = 128
BLK = 128
STRIDE = 256
SUMC = 8
NX = 4
NZ = 8
NH = 4
ND = 4
TOK = 256
WID = 512
ROWS = 64
HALF = ROWS // 2
HEADS = WID // HS
FSDP = NX * NZ
SCALE = 1.0 / math.sqrt(HS)
NEG = -1e30
MESH = pl.DeviceIdType.MESH
BF = jnp.bfloat16
F32 = jnp.float32


def place():
    d = lax.axis_index("dp")
    f = lax.axis_index("fsdp")
    h = lax.axis_index("head")
    return d, lax.div(f, NZ), lax.rem(f, NZ), h


def send(src, dst, ssem, rsem, dev):
    return pltpu.make_async_remote_copy(
        src_ref=src, dst_ref=dst, send_sem=ssem, recv_sem=rsem, device_id=dev, device_id_type=MESH
    )


def meet(bar, count, swapped):
    @pl.when(swapped)
    def _():
        pl.semaphore_wait(bar, count + 1)

    @pl.when(jnp.logical_not(swapped))
    def _():
        pl.semaphore_wait(bar, count)


class Links:
    def __init__(self):
        self.d, self.x, self.z, self.h = place()
        d, x, z, h = self.d, self.x, self.z, self.h
        self.xr, self.xl = lax.rem(x + 1, NX), lax.rem(x + NX - 1, NX)
        self.xo = lax.rem(x + 2, NX)
        self.zr, self.zl = lax.rem(z + 1, NZ), lax.rem(z + NZ - 1, NZ)
        f = x * NZ + z
        self.f = f
        self.sib = h + 1 - 2 * lax.rem(h, 2)
        self.rem = lax.rem(h + 2, NH)
        self.far = lax.rem(self.sib + 2, NH)
        self.dev_xr = (d, self.xr * NZ + z, h)
        self.dev_xl = (d, self.xl * NZ + z, h)
        self.dev_zr = (d, x * NZ + self.zr, h)
        self.dev_zl = (d, x * NZ + self.zl, h)
        self.dev_next = (d, lax.rem(f + 1, FSDP), h)
        self.dev_prev = (d, lax.rem(f + FSDP - 1, FSDP), h)
        self.dev_sib = (d, f, self.sib)
        self.dev_rem = (d, f, self.rem)
        self.dev_swap = (d, h * NZ + z, x)
        self.zs = [lax.rem(z + i, NZ) for i in range(NZ)]
        self.xs = [lax.rem(x + i, NX) for i in range(NX)]

    def dev_z(self, i):
        return (self.d, self.x * NZ + self.zs[i], self.h)

    def dev_x(self, i):
        return (self.d, self.xs[i] * NZ + self.z, self.h)


def vmem(n):
    return [pl.BlockSpec(memory_space=pltpu.VMEM)] * n


def dot_nt(a, b):
    return lax.dot_general(a, b, (((1,), (1,)), ((), ())), preferred_element_type=F32)


def dot_tn(a, b):
    return lax.dot_general(a, b, (((0,), (0,)), ((), ())), preferred_element_type=F32)


def dot_nn(a, b):
    return lax.dot_general(a, b, (((1,), (0,)), ((), ())), preferred_element_type=F32)


def step_kernel(
    w_ref, g_ref, q_ref, k_ref, v_ref, bias_ref,
    pown, pin, dq, dko, dvo, back, far, fin,
    wf, ga, qs, ks, vs, pk, pv, sa, sk, sv, wts, mxt, mx, pw, pp, gacc, gm, pfar, pmid, nb, ds,
    arm, bx, xrm, zin, zout, fout, sx, szo, szi,
    swap_sem, loc_sem, zr_s, zr_r, zl_s, zl_r, xr_s, xr_r, xl_s, xl_r, fr_s, fr_r, fl_s, fl_r,
    kv_s, kv_r, g_s, g_r, tz_s, tz_r, tx_s, tx_r,
    a_s, a_r, b_s, b_r, z_s, z_r, f_s, f_r, fl_sem, bk_s, bk_r, p_s, p_r, sx_s, sx_r, sz_s, sz_r,
):
    m = Links()
    d, x, z, h = m.d, m.x, m.z, m.h
    bar = pltpu.get_barrier_semaphore()

    def hello(dev):
        pl.semaphore_signal(bar, inc=1, device_id=dev, device_id_type=MESH)

    def owner(i):
        return (lax.rem(d + i, ND), h * NZ + z, x)

    swapped = x != h

    @pl.when(swapped)
    def _():
        hello(owner(0))

    hello(m.dev_rem)
    for i in range(1, ND):
        hello(owner(i))
    for i in range(1, NZ):
        hello(m.dev_z(i))
    for i in range(1, NX):
        hello(m.dev_x(i))
    hello(m.dev_sib)
    hello(m.dev_next)
    hello(m.dev_prev)
    local = [
        pltpu.make_async_copy(q_ref, qs, loc_sem.at[1]),
        pltpu.make_async_copy(k_ref, ks, loc_sem.at[2]),
        pltpu.make_async_copy(v_ref, vs, loc_sem.at[3]),
        pltpu.make_async_copy(g_ref, ga.at[h], loc_sem.at[4]),
        pltpu.make_async_copy(k_ref.at[pl.ds(TOK - SUMC, SUMC)], sa.at[x, z, 0], loc_sem.at[5]),
        pltpu.make_async_copy(v_ref.at[pl.ds(TOK - SUMC, SUMC)], sa.at[x, z, 1], loc_sem.at[6]),
    ]
    for c in local:
        c.start()
    meet(bar, (NZ - 1) + (NX - 1) + 4 + (ND - 1), swapped)

    def swap():
        return send(w_ref, wf.at[h, z], swap_sem.at[0], swap_sem.at[1], m.dev_swap)

    def stay():
        return pltpu.make_async_copy(w_ref, wf.at[x, z], loc_sem.at[0])

    @pl.when(swapped)
    def _():
        swap().start()

    @pl.when(jnp.logical_not(swapped))
    def _():
        stay().start()

    tz = []
    for i in range(1, NZ):
        for j, ref in enumerate((k_ref, v_ref)):
            c = send(
                ref.at[pl.ds(TOK - SUMC, SUMC)], sa.at[x, z, j], tz_s.at[j, i - 1], tz_r.at[j, i - 1], m.dev_z(i)
            )
            c.start()
            tz.append(c)
    kv = []
    for j, (ref, dst) in enumerate(((k_ref, pk), (v_ref, pv))):
        for i in range(TOK // ROWS):
            piece = pl.ds(i * ROWS, ROWS)
            kv.append(send(ref.at[piece], dst.at[piece], kv_s.at[j, i], kv_r.at[j, i], m.dev_next))
    kv[0].start()
    kv[1].start()
    g_sib = send(g_ref, ga.at[h], g_s.at[1], g_r.at[1], m.dev_sib)
    g_sib.start()
    g_rem = send(g_ref, ga.at[h], g_s.at[0], g_r.at[0], m.dev_rem)
    g_pass = send(ga.at[m.rem], ga.at[m.rem], g_s.at[2], g_r.at[2], m.dev_sib)

    @pl.when(swapped)
    def _():
        swap().wait_send()

    g_rem.start()

    @pl.when(swapped)
    def _():
        swap().wait_recv()

    @pl.when(jnp.logical_not(swapped))
    def _():
        stay().wait()

    order = [("own", 0), ("l", 1), ("r", 1), ("l", 2), ("r", 2), ("l", 3), ("r", 3), ("l", 4)]
    where = [z if kind == "own" else m.zs[NZ - s] if kind == "r" else m.zs[s] for kind, s in order]
    zrs, zls, xsd, xfd = {}, {}, {}, {}

    def zright(s):
        slot = wf.at[x, m.zs[(NZ - s) % NZ]]
        zrs[s] = send(slot, slot, zr_s.at[s], zr_r.at[s], m.dev_zr)
        zrs[s].start()

    def zleft(s):
        slot = wf.at[x, m.zs[s]]
        zls[s] = send(slot, slot, zl_s.at[s], zl_r.at[s], m.dev_zl)
        zls[s].start()

    def xsend(n):
        slot = wf.at[x, where[n]]
        xsd[n] = (
            send(slot, slot, xr_s.at[n], xr_r.at[n], m.dev_xr),
            send(slot, slot, xl_s.at[n], xl_r.at[n], m.dev_xl),
        )
        xsd[n][0].start()
        xsd[n][1].start()

    def arrive(n):
        kind, s = order[n]
        if kind == "own":
            zleft(0)
            zright(0)
            kv[2].start()
        elif kind == "r":
            zrs[s - 1].wait_recv()
            if s < 3:
                zright(s)
                kv[2 + s].start()
        else:
            zls[s - 1].wait_recv()
            if s < 4:
                zleft(s)
        xsend(n)

    def forward(n):
        a = wf.at[m.xl, where[n], pl.ds(0, HALF)]
        b = wf.at[m.xr, where[n], pl.ds(HALF, HALF)]
        xfd[n] = (
            send(a, a, fr_s.at[n], fr_r.at[n], m.dev_xr),
            send(b, b, fl_s.at[n], fl_r.at[n], m.dev_xl),
        )
        xsd[n][0].wait_recv()
        xfd[n][0].start()
        xsd[n][1].wait_recv()
        xfd[n][1].start()

    arrive(0)

    def fore(n):
        first = m.f == 0
        key_at = lax.broadcasted_iota(jnp.int32, (TOK, TOK), 0)
        query_at = lax.broadcasted_iota(jnp.int32, (TOK, TOK), 1)
        own_bias = jnp.where(key_at <= query_at, 0.0, NEG)
        low = jnp.where(query_at < BLK, 0, BLK) + jnp.where(first, 2 * TOK, 0)
        prior_bias = jnp.where(key_at >= low, 0.0, NEG)
        cols = pl.ds(n * HS, HS)
        q = qs[:, cols]
        keys = (pk[:, cols], ks[:, cols], sk[:, cols])
        values = (pv[:, cols], vs[:, cols], sv[:, cols])
        scores = [
            dot_nt(key, q) * SCALE + bias
            for key, bias in zip(keys, (prior_bias, own_bias, bias_ref[...]))
        ]
        peak = jnp.max(jnp.maximum(jnp.maximum(scores[0], scores[1]), scores[2]), axis=0, keepdims=True)
        raised = [jnp.exp(s - peak) for s in scores]
        scale = 1.0 / jnp.sum(raised[0] + raised[1] + raised[2], axis=0, keepdims=True)
        mixed_t = None
        for j in range(3):
            weight = raised[j] * scale
            wts[n, j] = weight
            term = dot_tn(values[j], weight.astype(BF))
            mixed_t = term if mixed_t is None else mixed_t + term
        mxt[cols, :] = mixed_t.astype(BF)
        mx[:, cols] = mixed_t.T.astype(BF)

    def hind(n):
        cols = pl.ds(n * HS, HS)
        q = qs[:, cols]
        keys = (pk[:, cols], ks[:, cols], sk[:, cols])
        values = (pv[:, cols], vs[:, cols], sv[:, cols])
        grad = gm[:, cols]
        delta = jnp.sum(grad.astype(F32).T * mxt[cols, :].astype(F32), axis=0, keepdims=True)
        dscore = [(wts[n, j] * (dot_nt(values[j], grad) - delta)).astype(BF) for j in range(3)]
        nb[0, n] = (dot_nn(dscore[0], q) * SCALE).astype(BF)
        nb[1, n] = dot_nn(wts[n, 0].astype(BF), grad).astype(BF)
        far_k = dot_nn(dscore[2], q) * SCALE
        ds[:, :, 0, :, cols] = far_k.reshape(NX, NZ, SUMC, HS).astype(BF)
        far_v = dot_nn(wts[n, 2].astype(BF), grad)
        ds[:, :, 1, :, cols] = far_v.reshape(NX, NZ, SUMC, HS).astype(BF)
        dko[:, cols] = dot_nn(dscore[1], q) * SCALE
        dvo[:, cols] = dot_nn(wts[n, 1].astype(BF), grad)
        dq_t = dot_tn(keys[0], dscore[0]) + dot_tn(keys[1], dscore[1]) + dot_tn(keys[2], dscore[2])
        dq[:, cols] = (dq_t.T * SCALE).astype(BF)

    arrive(1)
    arrive(2)
    forward(0)
    for c in local[4:]:
        c.wait()
    for c in tz:
        c.wait_recv()
    tx = []
    for i in range(1, NX):
        c = send(sa.at[x], sa.at[x], tx_s.at[i - 1], tx_r.at[i - 1], m.dev_x(i))
        c.start()
        tx.append(c)
    arrive(3)
    forward(1)
    arrive(4)
    for c in kv[5:]:
        c.start()
    forward(2)
    arrive(5)
    forward(3)
    arrive(6)
    forward(4)
    arrive(7)
    forward(5)
    for c in local[:3]:
        c.wait()
    g_rem.wait_recv()
    g_pass.start()
    for c in kv:
        c.wait_recv()
    for c in tx:
        c.wait_recv()
    sk[...] = sa[:, :, 0].astype(F32).reshape(TOK, WID).astype(BF)
    sv[...] = sa[:, :, 1].astype(F32).reshape(TOK, WID).astype(BF)
    fore(0)
    forward(6)
    fore(1)
    forward(7)
    fore(2)
    fore(3)

    def share(c):
        part = dot_nn(mxt[...], ga[c])
        pw[c] = part.astype(BF).reshape(NZ, ROWS, WID)

    rows = [m.zs[(i + 1) % NZ] for i in range(NZ)]

    def leg_a(n):
        r = rows[n]
        return (
            send(pw.at[m.xo, r, pl.ds(0, HALF)], arm.at[0, n], a_s.at[0, n], a_r.at[0, n], m.dev_xr),
            send(pw.at[m.xo, r, pl.ds(HALF, HALF)], arm.at[1, n], a_s.at[1, n], a_r.at[1, n], m.dev_xl),
        )

    def leg_b(n):
        return (
            send(bx.at[0, n], xrm.at[0, n], b_s.at[0, n], b_r.at[0, n], m.dev_xr),
            send(bx.at[1, n], xrm.at[1, n], b_s.at[1, n], b_r.at[1, n], m.dev_xl),
        )

    local[3].wait()
    g_sib.wait_recv()
    g_pass.wait_recv()
    share(m.xo)
    a_legs = [leg_a(n) for n in range(NZ)]
    for n in range(NZ):
        a_legs[n][0].start()
        a_legs[n][1].start()
    share(m.xr)
    share(m.xl)
    share(x)
    b_legs, z_legs = {}, {}

    def stage_b(n):
        r = rows[n]
        a_legs[n][0].wait_recv()
        bx[0, n, pl.ds(0, HALF)] = (
            arm[0, n].astype(F32) + pw[m.xr, r, pl.ds(0, HALF)].astype(F32)
        ).astype(BF)
        bx[0, n, pl.ds(HALF, HALF)] = pw[m.xr, r, pl.ds(HALF, HALF)]
        a_legs[n][1].wait_recv()
        bx[1, n, pl.ds(0, HALF)] = pw[m.xl, r, pl.ds(0, HALF)]
        bx[1, n, pl.ds(HALF, HALF)] = (
            arm[1, n].astype(F32) + pw[m.xl, r, pl.ds(HALF, HALF)].astype(F32)
        ).astype(BF)
        b_legs[n] = leg_b(n)
        b_legs[n][0].start()
        b_legs[n][1].start()

    def stage_z(n):
        b_legs[n][0].wait_recv()
        b_legs[n][1].wait_recv()
        zout[n] = (
            xrm[0, n].astype(F32) + xrm[1, n].astype(F32) + pw[x, rows[n]].astype(F32)
        ).astype(BF)
        if n < NZ - 1:
            z_legs[n] = send(zout.at[n], zin.at[n], z_s.at[n], z_r.at[n], m.dev_z(n + 1))
            z_legs[n].start()

    def wide(c):
        return wf[c].reshape(WID, WID)

    gacc[...] = dot_nt(ga[x], wide(x)) + dot_nt(ga[m.xr], wide(m.xr)) + dot_nt(ga[m.xl], wide(m.xl))
    for c in (x, m.xr, m.xl):
        pp[c] = dot_nn(mx[...], wide(c)).astype(BF)
    for n in range(NZ):
        xfd[n][0].wait_recv()
        xfd[n][1].wait_recv()
    gm[...] = (gacc[...] + dot_nt(ga[m.xo], wide(m.xo))).astype(BF)
    pp[m.xo] = dot_nn(mx[...], wide(m.xo)).astype(BF)
    p_legs = [
        send(pp.at[m.far], pfar, p_s.at[0], p_r.at[0], m.dev_sib),
        send(pp.at[m.sib], pin.at[0], p_s.at[1], p_r.at[1], m.dev_sib),
        send(pmid, pin.at[1], p_s.at[2], p_r.at[2], m.dev_rem),
    ]
    p_legs[0].start()
    p_legs[1].start()
    bk = []

    def neighbour(n):
        for j in range(2):
            c = send(nb.at[j, n], back.at[j, n], bk_s.at[j, n], bk_r.at[j, n], m.dev_prev)
            c.start()
            bk.append(c)

    hind(0)
    hind(1)
    neighbour(0)
    p_legs[0].wait_recv()
    pmid[...] = (pfar[...].astype(F32) + pp[m.rem].astype(F32)).astype(BF)
    hind(2)
    neighbour(1)
    p_legs[2].start()
    hind(3)
    neighbour(2)
    for n in range(NZ):
        stage_b(n)
    neighbour(3)
    s_legs = [
        send(ds.at[m.xs[i]], sx.at[i - 1], sx_s.at[i - 1], sx_r.at[i - 1], m.dev_x(i)) for i in range(1, NX)
    ]
    for c in s_legs:
        c.start()
    stage_z(0)
    stage_z(1)
    stage_z(2)
    stage_z(3)
    stage_z(4)
    stage_z(5)
    stage_z(6)
    stage_z(7)
    pown[...] = pp[h]
    for c in s_legs:
        c.wait_recv()
    szo[...] = (
        (ds[x].astype(F32) + sx[0].astype(F32)) + (sx[1].astype(F32) + sx[2].astype(F32))
    ).astype(BF)
    t_legs = [
        send(szo.at[m.zs[i]], szi.at[i - 1], sz_s.at[i - 1], sz_r.at[i - 1], m.dev_z(i)) for i in range(1, NZ)
    ]
    for c in t_legs:
        c.start()
    total = zout[NZ - 1].astype(F32)
    for n in range(NZ - 1):
        z_legs[n].wait_recv()
        total += zin[n].astype(F32)
    fout[...] = total.astype(BF)
    f_legs = [send(fout, fin.at[i], f_s.at[i], f_r.at[i], owner(i)) for i in range(ND)]

    def keep_own():
        return pltpu.make_async_copy(fout, fin.at[0], fl_sem)

    for i in range(1, ND):
        f_legs[i].start()

    @pl.when(swapped)
    def _():
        f_legs[0].start()

    @pl.when(jnp.logical_not(swapped))
    def _():
        keep_own().start()

    own = szo[z].astype(F32)
    for i in range(NZ - 1):
        t_legs[i].wait_recv()
        own += szi[i].astype(F32)
    far[...] = own
    for c in bk:
        c.wait()
    p_legs[1].wait_recv()
    p_legs[2].wait_recv()
    for c in tz + kv + [g_sib, g_rem, g_pass] + tx + s_legs + p_legs + t_legs:
        c.wait_send()
    for c in list(zrs.values()) + list(zls.values()) + list(z_legs.values()):
        c.wait_send()
    for n in range(NZ):
        for c in (*xsd[n], *xfd[n], *a_legs[n], *b_legs[n]):
            c.wait_send()
    for i in range(1, ND):
        f_legs[i].wait()

    @pl.when(swapped)
    def _():
        f_legs[0].wait()

    @pl.when(jnp.logical_not(swapped))
    def _():
        keep_own().wait()


def step(w, g, q, k, v, bias):
    dma = pltpu.SemaphoreType.DMA
    shape = jax.ShapeDtypeStruct
    hbm = [pl.BlockSpec(memory_space=pltpu.HBM)] * 5
    buf = pltpu.VMEM
    return pl.pallas_call(
        step_kernel,
        name="step",
        out_shape=(
            shape((TOK, WID), BF),
            shape((2, TOK, WID), BF),
            shape((TOK, WID), BF),
            shape((TOK, WID), F32),
            shape((TOK, WID), F32),
            shape((2, HEADS, TOK, HS), BF),
            shape((2, SUMC, WID), F32),
            shape((ND, ROWS, WID), BF),
        ),
        in_specs=hbm + vmem(1),
        out_specs=tuple(vmem(8)),
        scratch_shapes=[
            buf((NX, NZ, ROWS, WID), BF),
            buf((NH, TOK, WID), BF),
            buf((TOK, WID), BF),
            buf((TOK, WID), BF),
            buf((TOK, WID), BF),
            buf((TOK, WID), BF),
            buf((TOK, WID), BF),
            buf((NX, NZ, 2, SUMC, WID), BF),
            buf((TOK, WID), BF),
            buf((TOK, WID), BF),
            buf((HEADS, 3, TOK, TOK), F32),
            buf((WID, TOK), BF),
            buf((TOK, WID), BF),
            buf((NH, NZ, ROWS, WID), BF),
            buf((NH, TOK, WID), BF),
            buf((TOK, WID), F32),
            buf((TOK, WID), BF),
            buf((TOK, WID), BF),
            buf((TOK, WID), BF),
            buf((2, HEADS, TOK, HS), BF),
            buf((NX, NZ, 2, SUMC, WID), BF),
            buf((2, NZ, HALF, WID), BF),
            buf((2, NZ, ROWS, WID), BF),
            buf((2, NZ, ROWS, WID), BF),
            buf((NZ - 1, ROWS, WID), BF),
            buf((NZ, ROWS, WID), BF),
            buf((ROWS, WID), BF),
            buf((NX - 1, NZ, 2, SUMC, WID), BF),
            buf((NZ, 2, SUMC, WID), BF),
            buf((NZ - 1, 2, SUMC, WID), BF),
        ]
        + [dma((2,)), dma((7,))]
        + [dma((3,)), dma((3,)), dma((4,)), dma((4,))]
        + [dma((NZ,))] * 8
        + [dma((2, TOK // ROWS))] * 2
        + [dma((3,)), dma((3,))]
        + [dma((2, NZ - 1)), dma((2, NZ - 1)), dma((NX - 1,)), dma((NX - 1,))]
        + [dma((2, NZ))] * 4
        + [dma((NZ - 1,)), dma((NZ - 1,)), dma((ND,)), dma((ND,)), dma]
        + [dma((2, HEADS)), dma((2, HEADS)), dma((3,)), dma((3,))]
        + [dma((NX - 1,)), dma((NX - 1,)), dma((NZ - 1,)), dma((NZ - 1,))],
        compiler_params=pltpu.CompilerParams(
            collective_id=0, has_side_effects=True, vmem_limit_bytes=36 << 20
        ),
    )(*(pltpu.with_memory_space_constraint(a, pltpu.HBM) for a in (w, g, q, k, v)), bias)


def finish_kernel(pown, pin, dq, dko, dvo, back, far, fin, proj, qg, kg, vg, wg):
    proj[...] = (pown[...].astype(F32) + pin[0].astype(F32) + pin[1].astype(F32)).astype(BF)
    qg[...] = dq[...]
    for j, (out, mine) in enumerate(((kg, dko), (vg, dvo))):
        for n in range(HEADS):
            cols = pl.ds(n * HS, HS)
            out[pl.ds(0, TOK - 16), cols] = (
                mine[pl.ds(0, TOK - 16), cols] + back[j, n, pl.ds(0, TOK - 16)].astype(F32)
            ).astype(BF)
            tail = mine[pl.ds(TOK - 16, 16), cols] + back[j, n, pl.ds(TOK - 16, 16)].astype(F32)
            tail += jnp.concatenate([jnp.zeros((SUMC, HS), F32), far[j, :, cols]], axis=0)
            out[pl.ds(TOK - 16, 16), cols] = tail.astype(BF)
    wg[...] = (fin[0].astype(F32) + fin[1].astype(F32)) + (fin[2].astype(F32) + fin[3].astype(F32))


def finish(*parts):
    return pl.pallas_call(
        finish_kernel,
        name="finish",
        out_shape=(jax.ShapeDtypeStruct((TOK, WID), BF),) * 4 + (jax.ShapeDtypeStruct((ROWS, WID), F32),),
        in_specs=vmem(8),
        compiler_params=pltpu.CompilerParams(vmem_limit_bytes=16 << 20),
    )(*parts)


def body(queries, key_rows, value_rows, out_weight, sum_lists, out_grad):
    q, k, v, g = queries[0], key_rows[0], value_rows[0], out_grad[0]
    strides = jnp.arange(FSDP, dtype=jnp.int32)
    block = lax.axis_index("fsdp") * 2 + jnp.arange(2, dtype=jnp.int32)
    named = jnp.any(sum_lists[0][:, :, None] == strides[None, None, :], axis=1)
    usable = named & ((strides[None, :] + 1) * STRIDE <= (block[:, None] - 2) * BLK)
    bias = jnp.where(usable, 0.0, NEG).astype(F32)
    bias = jnp.broadcast_to(bias.T[:, None, :, None], (FSDP, SUMC, 2, BLK)).reshape(TOK, TOK)
    proj, qg, kg, vg, wg = finish(*step(out_weight, g, q, k, v, bias))
    return proj[None], qg[None], kg[None], vg[None], wg


def solution(mesh):
    tokens = P("dp", "fsdp", "head")
    return jax.shard_map(
        body,
        mesh=mesh,
        in_specs=(tokens, tokens, tokens, P("fsdp", "head"), P("dp", "fsdp", None), tokens),
        out_specs=(tokens, tokens, tokens, tokens, P("fsdp", "head")),
        check_vma=False,
    )
```

```python
import math

import jax
import jax.numpy as jnp
from jax import lax
from jax.experimental import pallas as pl
from jax.experimental.pallas import tpu as pltpu
from jax.sharding import PartitionSpec as P

HS = 128
BLK = 128
STRIDE = 256
SUMC = 8
NX = 4
NZ = 8
NH = 4
ND = 4
TOK = 256
WID = 512
ROWS = 64
HALF = ROWS // 2
HEADS = WID // HS
FSDP = NX * NZ
SCALE = 1.0 / math.sqrt(HS)
NEG = -1e30
MESH = pl.DeviceIdType.MESH
BF = jnp.bfloat16
F32 = jnp.float32


def place():
    d = lax.axis_index("dp")
    f = lax.axis_index("fsdp")
    h = lax.axis_index("head")
    return d, lax.div(f, NZ), lax.rem(f, NZ), h


def send(src, dst, ssem, rsem, dev):
    return pltpu.make_async_remote_copy(
        src_ref=src, dst_ref=dst, send_sem=ssem, recv_sem=rsem, device_id=dev, device_id_type=MESH
    )


def meet(bar, count, swapped):
    @pl.when(swapped)
    def _():
        pl.semaphore_wait(bar, count + 1)

    @pl.when(jnp.logical_not(swapped))
    def _():
        pl.semaphore_wait(bar, count)


class Links:
    def __init__(self):
        self.d, self.x, self.z, self.h = place()
        d, x, z, h = self.d, self.x, self.z, self.h
        self.xr, self.xl = lax.rem(x + 1, NX), lax.rem(x + NX - 1, NX)
        self.xo = lax.rem(x + 2, NX)
        self.zr, self.zl = lax.rem(z + 1, NZ), lax.rem(z + NZ - 1, NZ)
        f = x * NZ + z
        self.f = f
        self.sib = h + 1 - 2 * lax.rem(h, 2)
        self.rem = lax.rem(h + 2, NH)
        self.far = lax.rem(self.sib + 2, NH)
        self.dev_xr = (d, self.xr * NZ + z, h)
        self.dev_xl = (d, self.xl * NZ + z, h)
        self.dev_zr = (d, x * NZ + self.zr, h)
        self.dev_zl = (d, x * NZ + self.zl, h)
        self.dev_next = (d, lax.rem(f + 1, FSDP), h)
        self.dev_prev = (d, lax.rem(f + FSDP - 1, FSDP), h)
        self.dev_sib = (d, f, self.sib)
        self.dev_rem = (d, f, self.rem)
        self.dev_swap = (d, h * NZ + z, x)
        self.zs = [lax.rem(z + i, NZ) for i in range(NZ)]
        self.xs = [lax.rem(x + i, NX) for i in range(NX)]

    def dev_z(self, i):
        return (self.d, self.x * NZ + self.zs[i], self.h)

    def dev_x(self, i):
        return (self.d, self.xs[i] * NZ + self.z, self.h)


def vmem(n):
    return [pl.BlockSpec(memory_space=pltpu.VMEM)] * n


def dot_nt(a, b):
    return lax.dot_general(a, b, (((1,), (1,)), ((), ())), preferred_element_type=F32)


def dot_tn(a, b):
    return lax.dot_general(a, b, (((0,), (0,)), ((), ())), preferred_element_type=F32)


def dot_nn(a, b):
    return lax.dot_general(a, b, (((1,), (0,)), ((), ())), preferred_element_type=F32)


def step_kernel(
    w_ref, g_ref, q_ref, k_ref, v_ref, bias_ref,
    pown, pin, dq, dko, dvo, back, far, fin,
    wf, ga, qs, ks, vs, pk, pv, sa, sk, sv, wts, mxt, mx, pw, pp, gacc, gm, pfar, pmid, nb, ds,
    arm, bx, xrm, zin, zout, fout, sx, szo, szi,
    swap_sem, loc_sem, zr_s, zr_r, zl_s, zl_r, xr_s, xr_r, xl_s, xl_r, fr_s, fr_r, fl_s, fl_r,
    kv_s, kv_r, g_s, g_r, tz_s, tz_r, tx_s, tx_r,
    a_s, a_r, b_s, b_r, z_s, z_r, f_s, f_r, fl_sem, bk_s, bk_r, p_s, p_r, sx_s, sx_r, sz_s, sz_r,
):
    m = Links()
    d, x, z, h = m.d, m.x, m.z, m.h
    bar = pltpu.get_barrier_semaphore()

    def hello(dev):
        pl.semaphore_signal(bar, inc=1, device_id=dev, device_id_type=MESH)

    def owner(i):
        return (lax.rem(d + i, ND), h * NZ + z, x)

    swapped = x != h

    @pl.when(swapped)
    def _():
        hello(owner(0))

    hello(m.dev_rem)
    for i in range(1, ND):
        hello(owner(i))
    for i in range(1, NZ):
        hello(m.dev_z(i))
    for i in range(1, NX):
        hello(m.dev_x(i))
    hello(m.dev_sib)
    hello(m.dev_next)
    hello(m.dev_prev)
    local = [
        pltpu.make_async_copy(q_ref, qs, loc_sem.at[1]),
        pltpu.make_async_copy(k_ref, ks, loc_sem.at[2]),
        pltpu.make_async_copy(v_ref, vs, loc_sem.at[3]),
        pltpu.make_async_copy(g_ref, ga.at[h], loc_sem.at[4]),
        pltpu.make_async_copy(k_ref.at[pl.ds(TOK - SUMC, SUMC)], sa.at[x, z, 0], loc_sem.at[5]),
        pltpu.make_async_copy(v_ref.at[pl.ds(TOK - SUMC, SUMC)], sa.at[x, z, 1], loc_sem.at[6]),
    ]
    for c in local:
        c.start()
    meet(bar, (NZ - 1) + (NX - 1) + 4 + (ND - 1), swapped)

    def swap():
        return send(w_ref, wf.at[h, z], swap_sem.at[0], swap_sem.at[1], m.dev_swap)

    def stay():
        return pltpu.make_async_copy(w_ref, wf.at[x, z], loc_sem.at[0])

    @pl.when(swapped)
    def _():
        swap().start()

    @pl.when(jnp.logical_not(swapped))
    def _():
        stay().start()

    tz = []
    for i in range(1, NZ):
        for j, ref in enumerate((k_ref, v_ref)):
            c = send(
                ref.at[pl.ds(TOK - SUMC, SUMC)], sa.at[x, z, j], tz_s.at[j, i - 1], tz_r.at[j, i - 1], m.dev_z(i)
            )
            c.start()
            tz.append(c)
    kv = []
    for j, (ref, dst) in enumerate(((k_ref, pk), (v_ref, pv))):
        for i in range(TOK // ROWS):
            piece = pl.ds(i * ROWS, ROWS)
            kv.append(send(ref.at[piece], dst.at[piece], kv_s.at[j, i], kv_r.at[j, i], m.dev_next))
    kv[0].start()
    kv[1].start()
    kv[2].start()
    g_sib = send(g_ref, ga.at[h], g_s.at[1], g_r.at[1], m.dev_sib)
    g_sib.start()
    g_rem = send(g_ref, ga.at[h], g_s.at[0], g_r.at[0], m.dev_rem)
    g_pass = send(ga.at[m.rem], ga.at[m.rem], g_s.at[2], g_r.at[2], m.dev_sib)

    @pl.when(swapped)
    def _():
        swap().wait_send()

    g_rem.start()

    @pl.when(swapped)
    def _():
        swap().wait_recv()

    @pl.when(jnp.logical_not(swapped))
    def _():
        stay().wait()

    order = [("own", 0), ("l", 1), ("r", 1), ("l", 2), ("r", 2), ("l", 3), ("r", 3), ("l", 4)]
    where = [z if kind == "own" else m.zs[NZ - s] if kind == "r" else m.zs[s] for kind, s in order]
    zrs, zls, xsd, xfd = {}, {}, {}, {}

    def zright(s):
        slot = wf.at[x, m.zs[(NZ - s) % NZ]]
        zrs[s] = send(slot, slot, zr_s.at[s], zr_r.at[s], m.dev_zr)
        zrs[s].start()

    def zleft(s):
        slot = wf.at[x, m.zs[s]]
        zls[s] = send(slot, slot, zl_s.at[s], zl_r.at[s], m.dev_zl)
        zls[s].start()

    def xsend(n):
        slot = wf.at[x, where[n]]
        xsd[n] = (
            send(slot, slot, xr_s.at[n], xr_r.at[n], m.dev_xr),
            send(slot, slot, xl_s.at[n], xl_r.at[n], m.dev_xl),
        )
        xsd[n][0].start()
        xsd[n][1].start()

    def arrive(n):
        kind, s = order[n]
        if kind == "own":
            zleft(0)
            zright(0)
            kv[3].start()
        elif kind == "r":
            zrs[s - 1].wait_recv()
            if s < 3:
                zright(s)
                kv[3 + s].start()
        else:
            zls[s - 1].wait_recv()
            if s < 4:
                zleft(s)
        xsend(n)

    def forward(n):
        a = wf.at[m.xl, where[n], pl.ds(0, HALF)]
        b = wf.at[m.xr, where[n], pl.ds(HALF, HALF)]
        xfd[n] = (
            send(a, a, fr_s.at[n], fr_r.at[n], m.dev_xr),
            send(b, b, fl_s.at[n], fl_r.at[n], m.dev_xl),
        )
        xsd[n][0].wait_recv()
        xfd[n][0].start()
        xsd[n][1].wait_recv()
        xfd[n][1].start()

    arrive(0)

    def fore(n):
        first = m.f == 0
        key_at = lax.broadcasted_iota(jnp.int32, (TOK, TOK), 0)
        query_at = lax.broadcasted_iota(jnp.int32, (TOK, TOK), 1)
        own_bias = jnp.where(key_at <= query_at, 0.0, NEG)
        low = jnp.where(query_at < BLK, 0, BLK) + jnp.where(first, 2 * TOK, 0)
        prior_bias = jnp.where(key_at >= low, 0.0, NEG)
        cols = pl.ds(n * HS, HS)
        q = qs[:, cols]
        keys = (pk[:, cols], ks[:, cols], sk[:, cols])
        values = (pv[:, cols], vs[:, cols], sv[:, cols])
        scores = [
            dot_nt(key, q) * SCALE + bias
            for key, bias in zip(keys, (prior_bias, own_bias, bias_ref[...]))
        ]
        peak = jnp.max(jnp.maximum(jnp.maximum(scores[0], scores[1]), scores[2]), axis=0, keepdims=True)
        raised = [jnp.exp(s - peak) for s in scores]
        scale = 1.0 / jnp.sum(raised[0] + raised[1] + raised[2], axis=0, keepdims=True)
        mixed_t = None
        for j in range(3):
            weight = raised[j] * scale
            wts[n, j] = weight
            term = dot_tn(values[j], weight.astype(BF))
            mixed_t = term if mixed_t is None else mixed_t + term
        mxt[cols, :] = mixed_t.astype(BF)
        mx[:, cols] = mixed_t.T.astype(BF)

    def hind(n):
        cols = pl.ds(n * HS, HS)
        q = qs[:, cols]
        keys = (pk[:, cols], ks[:, cols], sk[:, cols])
        values = (pv[:, cols], vs[:, cols], sv[:, cols])
        grad = gm[:, cols]
        delta = jnp.sum(grad.astype(F32).T * mxt[cols, :].astype(F32), axis=0, keepdims=True)
        dscore = [(wts[n, j] * (dot_nt(values[j], grad) - delta)).astype(BF) for j in range(3)]
        nb[0, n] = (dot_nn(dscore[0], q) * SCALE).astype(BF)
        nb[1, n] = dot_nn(wts[n, 0].astype(BF), grad).astype(BF)
        far_k = dot_nn(dscore[2], q) * SCALE
        ds[:, :, 0, :, cols] = far_k.reshape(NX, NZ, SUMC, HS).astype(BF)
        far_v = dot_nn(wts[n, 2].astype(BF), grad)
        ds[:, :, 1, :, cols] = far_v.reshape(NX, NZ, SUMC, HS).astype(BF)
        dko[:, cols] = dot_nn(dscore[1], q) * SCALE
        dvo[:, cols] = dot_nn(wts[n, 1].astype(BF), grad)
        dq_t = dot_tn(keys[0], dscore[0]) + dot_tn(keys[1], dscore[1]) + dot_tn(keys[2], dscore[2])
        dq[:, cols] = (dq_t.T * SCALE).astype(BF)

    for c in local[4:]:
        c.wait()
    for c in tz:
        c.wait_recv()
    tx = []
    for i in range(1, NX):
        c = send(sa.at[x], sa.at[x], tx_s.at[i - 1], tx_r.at[i - 1], m.dev_x(i))
        c.start()
        tx.append(c)
    arrive(1)
    arrive(2)
    forward(0)
    arrive(3)
    arrive(4)
    for c in kv[6:]:
        c.start()
    forward(1)
    arrive(5)
    forward(2)
    arrive(6)
    forward(3)
    arrive(7)
    for c in local[:3]:
        c.wait()
    g_rem.wait_recv()
    g_pass.start()
    for c in kv:
        c.wait_recv()
    for c in tx:
        c.wait_recv()
    sk[...] = sa[:, :, 0].astype(F32).reshape(TOK, WID).astype(BF)
    sv[...] = sa[:, :, 1].astype(F32).reshape(TOK, WID).astype(BF)
    forward(4)
    fore(0)
    forward(5)
    fore(1)
    forward(6)
    fore(2)
    forward(7)
    fore(3)

    def share(c):
        part = dot_nn(mxt[...], ga[c])
        pw[c] = part.astype(BF).reshape(NZ, ROWS, WID)

    away = (4, 3, 5, 2, 6, 1, 7, 0)
    rows = [m.zs[i] for i in away]

    def leg_a(n):
        r = rows[n]
        return (
            send(pw.at[m.xo, r, pl.ds(0, HALF)], arm.at[0, n], a_s.at[0, n], a_r.at[0, n], m.dev_xr),
            send(pw.at[m.xo, r, pl.ds(HALF, HALF)], arm.at[1, n], a_s.at[1, n], a_r.at[1, n], m.dev_xl),
        )

    def leg_b(n):
        return (
            send(bx.at[0, n], xrm.at[0, n], b_s.at[0, n], b_r.at[0, n], m.dev_xr),
            send(bx.at[1, n], xrm.at[1, n], b_s.at[1, n], b_r.at[1, n], m.dev_xl),
        )

    local[3].wait()
    g_sib.wait_recv()
    g_pass.wait_recv()
    share(m.xo)
    a_legs = [leg_a(n) for n in range(NZ)]
    for n in range(NZ):
        a_legs[n][0].start()
        a_legs[n][1].start()
    share(m.xr)
    share(m.xl)
    share(x)
    b_legs, z_legs = {}, {}

    def stage_b(n):
        r = rows[n]
        a_legs[n][0].wait_recv()
        bx[0, n, pl.ds(0, HALF)] = (
            arm[0, n].astype(F32) + pw[m.xr, r, pl.ds(0, HALF)].astype(F32)
        ).astype(BF)
        bx[0, n, pl.ds(HALF, HALF)] = pw[m.xr, r, pl.ds(HALF, HALF)]
        a_legs[n][1].wait_recv()
        bx[1, n, pl.ds(0, HALF)] = pw[m.xl, r, pl.ds(0, HALF)]
        bx[1, n, pl.ds(HALF, HALF)] = (
            arm[1, n].astype(F32) + pw[m.xl, r, pl.ds(HALF, HALF)].astype(F32)
        ).astype(BF)
        b_legs[n] = leg_b(n)
        b_legs[n][0].start()
        b_legs[n][1].start()

    def stage_z(n):
        b_legs[n][0].wait_recv()
        b_legs[n][1].wait_recv()
        part = xrm[0, n].astype(F32) + xrm[1, n].astype(F32) + pw[x, rows[n]].astype(F32)
        if n == NZ - 1:
            return part
        zout[n] = part.astype(BF)
        z_legs[n] = send(zout.at[n], zin.at[n], z_s.at[n], z_r.at[n], m.dev_z(away[n]))
        z_legs[n].start()
        return None

    def wide(c):
        return wf[c].reshape(WID, WID)

    gacc[...] = dot_nt(ga[x], wide(x)) + dot_nt(ga[m.xr], wide(m.xr)) + dot_nt(ga[m.xl], wide(m.xl))
    for c in (x, m.xr, m.xl):
        pp[c] = dot_nn(mx[...], wide(c)).astype(BF)
    for n in range(NZ):
        xfd[n][0].wait_recv()
        xfd[n][1].wait_recv()
    gm[...] = (gacc[...] + dot_nt(ga[m.xo], wide(m.xo))).astype(BF)
    pp[m.xo] = dot_nn(mx[...], wide(m.xo)).astype(BF)
    p_legs = [
        send(pp.at[m.far], pfar, p_s.at[0], p_r.at[0], m.dev_sib),
        send(pp.at[m.sib], pin.at[0], p_s.at[1], p_r.at[1], m.dev_sib),
        send(pmid, pin.at[1], p_s.at[2], p_r.at[2], m.dev_rem),
    ]
    p_legs[0].start()
    p_legs[1].start()
    bk = []

    def neighbour(j, n):
        c = send(nb.at[j, n], back.at[j, n], bk_s.at[j, n], bk_r.at[j, n], m.dev_prev)
        c.start()
        bk.append(c)

    hind(0)
    hind(1)
    hind(2)
    hind(3)
    p_legs[0].wait_recv()
    pmid[...] = (pfar[...].astype(F32) + pp[m.rem].astype(F32)).astype(BF)
    for n in range(NZ):
        stage_b(n)
    p_legs[2].start()
    s_legs = [
        send(ds.at[m.xs[i]], sx.at[i - 1], sx_s.at[i - 1], sx_r.at[i - 1], m.dev_x(i)) for i in range(1, NX)
    ]
    for c in s_legs:
        c.start()
    for n in range(NZ - 1):
        stage_z(n)
    total = stage_z(NZ - 1)
    neighbour(0, 0)
    neighbour(1, 0)
    for n in range(NZ - 1):
        z_legs[n].wait_recv()
        total += zin[n].astype(F32)
    fout[...] = total.astype(BF)
    f_legs = [send(fout, fin.at[i], f_s.at[i], f_r.at[i], owner(i)) for i in range(ND)]

    def keep_own():
        return pltpu.make_async_copy(fout, fin.at[0], fl_sem)

    for i in range(1, ND):
        f_legs[i].start()

    @pl.when(swapped)
    def _():
        f_legs[0].start()

    @pl.when(jnp.logical_not(swapped))
    def _():
        keep_own().start()

    pown[...] = pp[h]
    for c in s_legs:
        c.wait_recv()
    szo[...] = (
        (ds[x].astype(F32) + sx[0].astype(F32)) + (sx[1].astype(F32) + sx[2].astype(F32))
    ).astype(BF)
    t_legs = [
        send(szo.at[m.zs[i]], szi.at[i - 1], sz_s.at[i - 1], sz_r.at[i - 1], m.dev_z(i)) for i in range(1, NZ)
    ]
    for c in t_legs:
        c.start()
    for n in range(1, HEADS):
        neighbour(0, n)
        neighbour(1, n)
    own = szo[z].astype(F32)
    for i in range(NZ - 1):
        t_legs[i].wait_recv()
        own += szi[i].astype(F32)
    far[...] = own
    for c in bk:
        c.wait()
    p_legs[1].wait_recv()
    p_legs[2].wait_recv()
    for c in tz + kv + [g_sib, g_rem, g_pass] + tx + s_legs + p_legs + t_legs:
        c.wait_send()
    for c in list(zrs.values()) + list(zls.values()) + list(z_legs.values()):
        c.wait_send()
    for n in range(NZ):
        for c in (*xsd[n], *xfd[n], *a_legs[n], *b_legs[n]):
            c.wait_send()
    for i in range(1, ND):
        f_legs[i].wait()

    @pl.when(swapped)
    def _():
        f_legs[0].wait()

    @pl.when(jnp.logical_not(swapped))
    def _():
        keep_own().wait()


def step(w, g, q, k, v, bias):
    dma = pltpu.SemaphoreType.DMA
    shape = jax.ShapeDtypeStruct
    hbm = [pl.BlockSpec(memory_space=pltpu.HBM)] * 5
    buf = pltpu.VMEM
    return pl.pallas_call(
        step_kernel,
        name="step",
        out_shape=(
            shape((TOK, WID), BF),
            shape((2, TOK, WID), BF),
            shape((TOK, WID), BF),
            shape((TOK, WID), F32),
            shape((TOK, WID), F32),
            shape((2, HEADS, TOK, HS), BF),
            shape((2, SUMC, WID), F32),
            shape((ND, ROWS, WID), BF),
        ),
        in_specs=hbm + vmem(1),
        out_specs=tuple(vmem(8)),
        scratch_shapes=[
            buf((NX, NZ, ROWS, WID), BF),
            buf((NH, TOK, WID), BF),
            buf((TOK, WID), BF),
            buf((TOK, WID), BF),
            buf((TOK, WID), BF),
            buf((TOK, WID), BF),
            buf((TOK, WID), BF),
            buf((NX, NZ, 2, SUMC, WID), BF),
            buf((TOK, WID), BF),
            buf((TOK, WID), BF),
            buf((HEADS, 3, TOK, TOK), F32),
            buf((WID, TOK), BF),
            buf((TOK, WID), BF),
            buf((NH, NZ, ROWS, WID), BF),
            buf((NH, TOK, WID), BF),
            buf((TOK, WID), F32),
            buf((TOK, WID), BF),
            buf((TOK, WID), BF),
            buf((TOK, WID), BF),
            buf((2, HEADS, TOK, HS), BF),
            buf((NX, NZ, 2, SUMC, WID), BF),
            buf((2, NZ, HALF, WID), BF),
            buf((2, NZ, ROWS, WID), BF),
            buf((2, NZ, ROWS, WID), BF),
            buf((NZ - 1, ROWS, WID), BF),
            buf((NZ - 1, ROWS, WID), BF),
            buf((ROWS, WID), BF),
            buf((NX - 1, NZ, 2, SUMC, WID), BF),
            buf((NZ, 2, SUMC, WID), BF),
            buf((NZ - 1, 2, SUMC, WID), BF),
        ]
        + [dma((2,)), dma((7,))]
        + [dma((3,)), dma((3,)), dma((4,)), dma((4,))]
        + [dma((NZ,))] * 8
        + [dma((2, TOK // ROWS))] * 2
        + [dma((3,)), dma((3,))]
        + [dma((2, NZ - 1)), dma((2, NZ - 1)), dma((NX - 1,)), dma((NX - 1,))]
        + [dma((2, NZ))] * 4
        + [dma((NZ - 1,)), dma((NZ - 1,)), dma((ND,)), dma((ND,)), dma]
        + [dma((2, HEADS)), dma((2, HEADS)), dma((3,)), dma((3,))]
        + [dma((NX - 1,)), dma((NX - 1,)), dma((NZ - 1,)), dma((NZ - 1,))],
        compiler_params=pltpu.CompilerParams(
            collective_id=0, has_side_effects=True, vmem_limit_bytes=36 << 20
        ),
    )(*(pltpu.with_memory_space_constraint(a, pltpu.HBM) for a in (w, g, q, k, v)), bias)


def finish_kernel(pown, pin, dq, dko, dvo, back, far, fin, proj, qg, kg, vg, wg):
    proj[...] = (pown[...].astype(F32) + pin[0].astype(F32) + pin[1].astype(F32)).astype(BF)
    qg[...] = dq[...]
    for j, (out, mine) in enumerate(((kg, dko), (vg, dvo))):
        for n in range(HEADS):
            cols = pl.ds(n * HS, HS)
            out[pl.ds(0, TOK - 16), cols] = (
                mine[pl.ds(0, TOK - 16), cols] + back[j, n, pl.ds(0, TOK - 16)].astype(F32)
            ).astype(BF)
            tail = mine[pl.ds(TOK - 16, 16), cols] + back[j, n, pl.ds(TOK - 16, 16)].astype(F32)
            tail += jnp.concatenate([jnp.zeros((SUMC, HS), F32), far[j, :, cols]], axis=0)
            out[pl.ds(TOK - 16, 16), cols] = tail.astype(BF)
    wg[...] = (fin[0].astype(F32) + fin[1].astype(F32)) + (fin[2].astype(F32) + fin[3].astype(F32))


def finish(*parts):
    return pl.pallas_call(
        finish_kernel,
        name="finish",
        out_shape=(jax.ShapeDtypeStruct((TOK, WID), BF),) * 4 + (jax.ShapeDtypeStruct((ROWS, WID), F32),),
        in_specs=vmem(8),
        compiler_params=pltpu.CompilerParams(vmem_limit_bytes=16 << 20),
    )(*parts)


def body(queries, key_rows, value_rows, out_weight, sum_lists, out_grad):
    q, k, v, g = queries[0], key_rows[0], value_rows[0], out_grad[0]
    strides = jnp.arange(FSDP, dtype=jnp.int32)
    block = lax.axis_index("fsdp") * 2 + jnp.arange(2, dtype=jnp.int32)
    named = jnp.any(sum_lists[0][:, :, None] == strides[None, None, :], axis=1)
    usable = named & ((strides[None, :] + 1) * STRIDE <= (block[:, None] - 2) * BLK)
    bias = jnp.where(usable, 0.0, NEG).astype(F32)
    bias = jnp.broadcast_to(bias.T[:, None, :, None], (FSDP, SUMC, 2, BLK)).reshape(TOK, TOK)
    proj, qg, kg, vg, wg = finish(*step(out_weight, g, q, k, v, bias))
    return proj[None], qg[None], kg[None], vg[None], wg


def solution(mesh):
    tokens = P("dp", "fsdp", "head")
    return jax.shard_map(
        body,
        mesh=mesh,
        in_specs=(tokens, tokens, tokens, P("fsdp", "head"), P("dp", "fsdp", None), tokens),
        out_specs=(tokens, tokens, tokens, tokens, P("fsdp", "head")),
        check_vma=False,
    )
```

```python
import math

import jax
import jax.numpy as jnp
from jax import lax
from jax.experimental import pallas as pl
from jax.experimental.pallas import tpu as pltpu
from jax.sharding import PartitionSpec as P

HS = 128
BLK = 128
STRIDE = 256
SUMC = 8
NX = 4
NZ = 8
NH = 4
ND = 4
TOK = 256
WID = 512
ROWS = 64
HALF = ROWS // 2
HEADS = WID // HS
FSDP = NX * NZ
SCALE = 1.0 / math.sqrt(HS)
NEG = -1e30
MESH = pl.DeviceIdType.MESH
BF = jnp.bfloat16
F32 = jnp.float32


def place():
    d = lax.axis_index("dp")
    f = lax.axis_index("fsdp")
    h = lax.axis_index("head")
    return d, lax.div(f, NZ), lax.rem(f, NZ), h


def send(src, dst, ssem, rsem, dev):
    return pltpu.make_async_remote_copy(
        src_ref=src, dst_ref=dst, send_sem=ssem, recv_sem=rsem, device_id=dev, device_id_type=MESH
    )


def meet(bar, count, swapped):
    @pl.when(swapped)
    def _():
        pl.semaphore_wait(bar, count + 1)

    @pl.when(jnp.logical_not(swapped))
    def _():
        pl.semaphore_wait(bar, count)


class Links:
    def __init__(self):
        self.d, self.x, self.z, self.h = place()
        d, x, z, h = self.d, self.x, self.z, self.h
        self.xr, self.xl = lax.rem(x + 1, NX), lax.rem(x + NX - 1, NX)
        self.xo = lax.rem(x + 2, NX)
        self.zr, self.zl = lax.rem(z + 1, NZ), lax.rem(z + NZ - 1, NZ)
        f = x * NZ + z
        self.f = f
        self.sib = h + 1 - 2 * lax.rem(h, 2)
        self.rem = lax.rem(h + 2, NH)
        self.far = lax.rem(self.sib + 2, NH)
        self.dev_xr = (d, self.xr * NZ + z, h)
        self.dev_xl = (d, self.xl * NZ + z, h)
        self.dev_zr = (d, x * NZ + self.zr, h)
        self.dev_zl = (d, x * NZ + self.zl, h)
        self.dev_next = (d, lax.rem(f + 1, FSDP), h)
        self.dev_prev = (d, lax.rem(f + FSDP - 1, FSDP), h)
        self.dev_sib = (d, f, self.sib)
        self.dev_rem = (d, f, self.rem)
        self.dev_swap = (d, h * NZ + z, x)
        self.zs = [lax.rem(z + i, NZ) for i in range(NZ)]
        self.xs = [lax.rem(x + i, NX) for i in range(NX)]

    def dev_z(self, i):
        return (self.d, self.x * NZ + self.zs[i], self.h)

    def dev_x(self, i):
        return (self.d, self.xs[i] * NZ + self.z, self.h)


def vmem(n):
    return [pl.BlockSpec(memory_space=pltpu.VMEM)] * n


def dot_nt(a, b):
    return lax.dot_general(a, b, (((1,), (1,)), ((), ())), preferred_element_type=F32)


def dot_tn(a, b):
    return lax.dot_general(a, b, (((0,), (0,)), ((), ())), preferred_element_type=F32)


def dot_nn(a, b):
    return lax.dot_general(a, b, (((1,), (0,)), ((), ())), preferred_element_type=F32)


def step_kernel(
    w_ref, g_ref, q_ref, k_ref, v_ref, bias_ref,
    pown, pin, dq, dko, dvo, back, far, fin,
    wf, ga, qs, ks, vs, pk, pv, sa, sk, sv, wts, mxt, mx, pw, pp, gacc, gm, pfar, pmid, nb, ds,
    arm, bx, xrm, zin, zout, fout, sx, szo, szi, rv,
    swap_sem, loc_sem, zr_s, zr_r, zl_s, zl_r, xr_s, xr_r, xl_s, xl_r, fr_s, fr_r, fl_s, fl_r,
    kv_s, kv_r, g_s, g_r, tr_s, tr_r, tl_s, tl_r, tx_s, tx_r, rv_s, rv_r, rf_s,
    a_s, a_r, b_s, b_r, z_s, z_r, f_s, f_r, fl_sem, bk_s, bk_r, p_s, p_r, sx_s, sx_r, sz_s, sz_r,
):
    m = Links()
    d, x, z, h = m.d, m.x, m.z, m.h
    bar = pltpu.get_barrier_semaphore()

    def hello(dev):
        pl.semaphore_signal(bar, inc=1, device_id=dev, device_id_type=MESH)

    def owner(i):
        return (lax.rem(d + i, ND), h * NZ + z, x)

    swapped = x != h

    @pl.when(swapped)
    def _():
        hello(owner(0))

    hello(m.dev_rem)
    for i in range(1, ND):
        hello(owner(i))
    for i in range(1, NZ):
        hello(m.dev_z(i))
    for i in range(1, NX):
        hello(m.dev_x(i))
    hello(m.dev_sib)
    hello(m.dev_next)
    hello(m.dev_prev)
    local = [
        pltpu.make_async_copy(q_ref, qs, loc_sem.at[1]),
        pltpu.make_async_copy(k_ref, ks, loc_sem.at[2]),
        pltpu.make_async_copy(v_ref, vs, loc_sem.at[3]),
        pltpu.make_async_copy(g_ref, ga.at[h], loc_sem.at[4]),
        pltpu.make_async_copy(k_ref.at[pl.ds(TOK - SUMC, SUMC)], sa.at[x, z, 0], loc_sem.at[5]),
        pltpu.make_async_copy(v_ref.at[pl.ds(TOK - SUMC, SUMC)], sa.at[x, z, 1], loc_sem.at[6]),
    ]
    for c in local:
        c.start()
    meet(bar, (NZ - 1) + (NX - 1) + 4 + (ND - 1), swapped)

    def swap():
        return send(w_ref, wf.at[h, z], swap_sem.at[0], swap_sem.at[1], m.dev_swap)

    def stay():
        return pltpu.make_async_copy(w_ref, wf.at[x, z], loc_sem.at[0])

    @pl.when(swapped)
    def _():
        swap().start()

    @pl.when(jnp.logical_not(swapped))
    def _():
        stay().start()

    tx = []
    for i in range(1, NX):
        for j, ref in enumerate((k_ref, v_ref)):
            c = send(
                ref.at[pl.ds(TOK - SUMC, SUMC)], sa.at[x, z, j], tx_s.at[j, i - 1], tx_r.at[j, i - 1], m.dev_x(i)
            )
            c.start()
            tx.append(c)
    kv = []
    for j, (ref, dst) in enumerate(((k_ref, pk), (v_ref, pv))):
        for i in range(TOK // ROWS):
            piece = pl.ds(i * ROWS, ROWS)
            kv.append(send(ref.at[piece], dst.at[piece], kv_s.at[j, i], kv_r.at[j, i], m.dev_next))
    wraps = z == NZ - 1
    pieces = [pl.ds(i * ROWS, ROWS) for i in range(TOK // ROWS)]
    hop = [send(v_ref.at[p], rv.at[p], rv_s.at[i], rv_r.at[i], m.dev_xr) for i, p in enumerate(pieces)]
    hand = [send(rv.at[p], pv.at[p], rf_s.at[i], kv_r.at[1, i], m.dev_zr) for i, p in enumerate(pieces)]

    @pl.when(wraps)
    def _():
        for c in hop:
            c.start()

    def values(i):
        @pl.when(jnp.logical_not(wraps))
        def _():
            kv[4 + i].start()

    def hand_on(i):
        @pl.when(wraps)
        def _():
            hop[i].wait_recv()
            hand[i].start()

    kv[0].start()
    kv[1].start()
    kv[2].start()
    g_sib = send(g_ref, ga.at[h], g_s.at[1], g_r.at[1], m.dev_sib)
    g_sib.start()
    g_rem = send(g_ref, ga.at[h], g_s.at[0], g_r.at[0], m.dev_rem)
    g_pass = send(ga.at[m.rem], ga.at[m.rem], g_s.at[2], g_r.at[2], m.dev_sib)

    @pl.when(swapped)
    def _():
        swap().wait_send()

    g_rem.start()

    @pl.when(swapped)
    def _():
        swap().wait_recv()

    @pl.when(jnp.logical_not(swapped))
    def _():
        stay().wait()

    order = [("own", 0), ("l", 1), ("r", 1), ("l", 2), ("r", 2), ("l", 3), ("r", 3), ("l", 4)]
    where = [z if kind == "own" else m.zs[NZ - s] if kind == "r" else m.zs[s] for kind, s in order]
    zrs, zls, xsd, xfd = {}, {}, {}, {}

    tzr, tzl = {}, {}

    def zright(s):
        at = m.zs[(NZ - s) % NZ]
        slot = wf.at[x, at]
        zrs[s] = send(slot, slot, zr_s.at[s], zr_r.at[s], m.dev_zr)
        zrs[s].start()
        slab = sa.at[:, at]
        tzr[s] = send(slab, slab, tr_s.at[s], tr_r.at[s], m.dev_zr)

    def zleft(s):
        at = m.zs[s]
        slot = wf.at[x, at]
        zls[s] = send(slot, slot, zl_s.at[s], zl_r.at[s], m.dev_zl)
        zls[s].start()
        slab = sa.at[:, at]
        tzl[s] = send(slab, slab, tl_s.at[s], tl_r.at[s], m.dev_zl)

    def xsend(n):
        slot = wf.at[x, where[n]]
        xsd[n] = (
            send(slot, slot, xr_s.at[n], xr_r.at[n], m.dev_xr),
            send(slot, slot, xl_s.at[n], xl_r.at[n], m.dev_xl),
        )
        xsd[n][0].start()
        xsd[n][1].start()

    def arrive(n):
        kind, s = order[n]
        if kind == "own":
            zleft(0)
            zright(0)
        elif kind == "r":
            zrs[s - 1].wait_recv()
            if s < 3:
                zright(s)
        else:
            zls[s - 1].wait_recv()
            if s < 4:
                zleft(s)
        xsend(n)

    def summaries(n):
        kind, s = order[n]
        if kind == "own":
            for c in local[4:]:
                c.wait()
            for c in tx:
                c.wait_recv()
            tzl[0].start()
            tzr[0].start()
            kv[3].start()
        elif kind == "r":
            tzr[s - 1].wait_recv()
            if s < 3:
                tzr[s].start()
                values(s - 1)
        else:
            tzl[s - 1].wait_recv()
            if s < 4:
                tzl[s].start()

    def forward(n):
        a = wf.at[m.xl, where[n], pl.ds(0, HALF)]
        b = wf.at[m.xr, where[n], pl.ds(HALF, HALF)]
        xfd[n] = (
            send(a, a, fr_s.at[n], fr_r.at[n], m.dev_xr),
            send(b, b, fl_s.at[n], fl_r.at[n], m.dev_xl),
        )
        xsd[n][0].wait_recv()
        xfd[n][0].start()
        xsd[n][1].wait_recv()
        xfd[n][1].start()

    arrive(0)

    def fore(n):
        first = m.f == 0
        key_at = lax.broadcasted_iota(jnp.int32, (TOK, TOK), 0)
        query_at = lax.broadcasted_iota(jnp.int32, (TOK, TOK), 1)
        own_bias = jnp.where(key_at <= query_at, 0.0, NEG)
        low = jnp.where(query_at < BLK, 0, BLK) + jnp.where(first, 2 * TOK, 0)
        prior_bias = jnp.where(key_at >= low, 0.0, NEG)
        cols = pl.ds(n * HS, HS)
        q = qs[:, cols]
        keys = (pk[:, cols], ks[:, cols], sk[:, cols])
        values = (pv[:, cols], vs[:, cols], sv[:, cols])
        scores = [
            dot_nt(key, q) * SCALE + bias
            for key, bias in zip(keys, (prior_bias, own_bias, bias_ref[...]))
        ]
        peak = jnp.max(jnp.maximum(jnp.maximum(scores[0], scores[1]), scores[2]), axis=0, keepdims=True)
        raised = [jnp.exp(s - peak) for s in scores]
        scale = 1.0 / jnp.sum(raised[0] + raised[1] + raised[2], axis=0, keepdims=True)
        mixed_t = None
        for j in range(3):
            weight = raised[j] * scale
            wts[n, j] = weight
            term = dot_tn(values[j], weight.astype(BF))
            mixed_t = term if mixed_t is None else mixed_t + term
        mxt[cols, :] = mixed_t.astype(BF)
        mx[:, cols] = mixed_t.T.astype(BF)

    def hind(n):
        cols = pl.ds(n * HS, HS)
        q = qs[:, cols]
        keys = (pk[:, cols], ks[:, cols], sk[:, cols])
        values = (pv[:, cols], vs[:, cols], sv[:, cols])
        grad = gm[:, cols]
        delta = jnp.sum(grad.astype(F32).T * mxt[cols, :].astype(F32), axis=0, keepdims=True)
        dscore = [(wts[n, j] * (dot_nt(values[j], grad) - delta)).astype(BF) for j in range(3)]
        nb[0, n] = (dot_nn(dscore[0], q) * SCALE).astype(BF)
        nb[1, n] = dot_nn(wts[n, 0].astype(BF), grad).astype(BF)
        far_k = dot_nn(dscore[2], q) * SCALE
        ds[:, :, 0, :, cols] = far_k.reshape(NX, NZ, SUMC, HS).astype(BF)
        far_v = dot_nn(wts[n, 2].astype(BF), grad)
        ds[:, :, 1, :, cols] = far_v.reshape(NX, NZ, SUMC, HS).astype(BF)
        dko[:, cols] = dot_nn(dscore[1], q) * SCALE
        dvo[:, cols] = dot_nn(wts[n, 1].astype(BF), grad)
        dq_t = dot_tn(keys[0], dscore[0]) + dot_tn(keys[1], dscore[1]) + dot_tn(keys[2], dscore[2])
        dq[:, cols] = (dq_t.T * SCALE).astype(BF)

    summaries(0)
    hand_on(0)
    hand_on(1)
    arrive(1)
    arrive(2)
    hand_on(2)
    hand_on(3)
    summaries(1)
    summaries(2)
    forward(0)
    arrive(3)
    arrive(4)
    forward(1)
    summaries(3)
    summaries(4)
    values(2)
    values(3)
    arrive(5)
    forward(2)
    arrive(6)
    forward(3)
    summaries(5)
    summaries(6)
    arrive(7)
    forward(4)
    for c in local[:3]:
        c.wait()
    g_rem.wait_recv()
    g_pass.start()
    summaries(7)
    for c in kv:
        c.wait_recv()
    sk[...] = sa[:, :, 0].astype(F32).reshape(TOK, WID).astype(BF)
    sv[...] = sa[:, :, 1].astype(F32).reshape(TOK, WID).astype(BF)
    fore(0)
    forward(5)
    fore(1)
    forward(6)
    fore(2)
    forward(7)
    fore(3)

    def share(c):
        part = dot_nn(mxt[...], ga[c])
        pw[c] = part.astype(BF).reshape(NZ, ROWS, WID)

    away = (4, 3, 5, 2, 6, 1, 7, 0)
    rows = [m.zs[i] for i in away]

    def leg_a(n):
        r = rows[n]
        return (
            send(pw.at[m.xo, r, pl.ds(0, HALF)], arm.at[0, n], a_s.at[0, n], a_r.at[0, n], m.dev_xr),
            send(pw.at[m.xo, r, pl.ds(HALF, HALF)], arm.at[1, n], a_s.at[1, n], a_r.at[1, n], m.dev_xl),
        )

    def leg_b(n):
        return (
            send(bx.at[0, n], xrm.at[0, n], b_s.at[0, n], b_r.at[0, n], m.dev_xr),
            send(bx.at[1, n], xrm.at[1, n], b_s.at[1, n], b_r.at[1, n], m.dev_xl),
        )

    local[3].wait()
    g_sib.wait_recv()
    g_pass.wait_recv()
    share(m.xo)
    a_legs = [leg_a(n) for n in range(NZ)]
    for n in range(NZ):
        a_legs[n][0].start()
        a_legs[n][1].start()
    share(m.xr)
    share(m.xl)
    share(x)
    b_legs, z_legs = {}, {}

    def stage_b(n):
        r = rows[n]
        a_legs[n][0].wait_recv()
        bx[0, n, pl.ds(0, HALF)] = (
            arm[0, n].astype(F32) + pw[m.xr, r, pl.ds(0, HALF)].astype(F32)
        ).astype(BF)
        bx[0, n, pl.ds(HALF, HALF)] = pw[m.xr, r, pl.ds(HALF, HALF)]
        a_legs[n][1].wait_recv()
        bx[1, n, pl.ds(0, HALF)] = pw[m.xl, r, pl.ds(0, HALF)]
        bx[1, n, pl.ds(HALF, HALF)] = (
            arm[1, n].astype(F32) + pw[m.xl, r, pl.ds(HALF, HALF)].astype(F32)
        ).astype(BF)
        b_legs[n] = leg_b(n)
        b_legs[n][0].start()
        b_legs[n][1].start()

    def stage_z(n):
        b_legs[n][0].wait_recv()
        b_legs[n][1].wait_recv()
        part = xrm[0, n].astype(F32) + xrm[1, n].astype(F32) + pw[x, rows[n]].astype(F32)
        if n == NZ - 1:
            return part
        zout[n] = part.astype(BF)
        z_legs[n] = send(zout.at[n], zin.at[n], z_s.at[n], z_r.at[n], m.dev_z(away[n]))
        z_legs[n].start()
        return None

    def wide(c):
        return wf[c].reshape(WID, WID)

    gacc[...] = dot_nt(ga[x], wide(x)) + dot_nt(ga[m.xr], wide(m.xr)) + dot_nt(ga[m.xl], wide(m.xl))
    for c in (x, m.xr, m.xl):
        pp[c] = dot_nn(mx[...], wide(c)).astype(BF)
    for n in range(NZ):
        xfd[n][0].wait_recv()
        xfd[n][1].wait_recv()
    gm[...] = (gacc[...] + dot_nt(ga[m.xo], wide(m.xo))).astype(BF)
    pp[m.xo] = dot_nn(mx[...], wide(m.xo)).astype(BF)
    p_legs = [
        send(pp.at[m.far], pfar, p_s.at[0], p_r.at[0], m.dev_sib),
        send(pp.at[m.sib], pin.at[0], p_s.at[1], p_r.at[1], m.dev_sib),
        send(pmid, pin.at[1], p_s.at[2], p_r.at[2], m.dev_rem),
    ]
    p_legs[0].start()
    p_legs[1].start()
    bk = []

    def neighbour(j, n):
        c = send(nb.at[j, n], back.at[j, n], bk_s.at[j, n], bk_r.at[j, n], m.dev_prev)
        c.start()
        bk.append(c)

    hind(0)
    hind(1)
    hind(2)
    hind(3)
    p_legs[0].wait_recv()
    pmid[...] = (pfar[...].astype(F32) + pp[m.rem].astype(F32)).astype(BF)
    for n in range(NZ):
        stage_b(n)
    p_legs[2].start()
    s_legs = [
        send(ds.at[m.xs[i]], sx.at[i - 1], sx_s.at[i - 1], sx_r.at[i - 1], m.dev_x(i)) for i in range(1, NX)
    ]
    for c in s_legs:
        c.start()
    for n in range(NZ - 1):
        stage_z(n)
    total = stage_z(NZ - 1)
    neighbour(0, 0)
    neighbour(1, 0)
    for n in range(NZ - 1):
        z_legs[n].wait_recv()
        total += zin[n].astype(F32)
    fout[...] = total.astype(BF)
    f_legs = [send(fout, fin.at[i], f_s.at[i], f_r.at[i], owner(i)) for i in range(ND)]

    def keep_own():
        return pltpu.make_async_copy(fout, fin.at[0], fl_sem)

    for i in range(1, ND):
        f_legs[i].start()

    @pl.when(swapped)
    def _():
        f_legs[0].start()

    @pl.when(jnp.logical_not(swapped))
    def _():
        keep_own().start()

    pown[...] = pp[h]
    for c in s_legs:
        c.wait_recv()
    szo[...] = (
        (ds[x].astype(F32) + sx[0].astype(F32)) + (sx[1].astype(F32) + sx[2].astype(F32))
    ).astype(BF)
    t_legs = [
        send(szo.at[m.zs[i]], szi.at[i - 1], sz_s.at[i - 1], sz_r.at[i - 1], m.dev_z(i)) for i in range(1, NZ)
    ]
    for c in t_legs:
        c.start()
    for n in range(1, HEADS):
        neighbour(0, n)
        neighbour(1, n)
    own = szo[z].astype(F32)
    for i in range(NZ - 1):
        t_legs[i].wait_recv()
        own += szi[i].astype(F32)
    far[...] = own
    for c in bk:
        c.wait()
    p_legs[1].wait_recv()
    p_legs[2].wait_recv()
    for c in tx + kv[:4] + [g_sib, g_rem, g_pass] + s_legs + p_legs + t_legs:
        c.wait_send()
    for c in list(tzr.values()) + list(tzl.values()):
        c.wait_send()

    @pl.when(wraps)
    def _():
        for c in hop + hand:
            c.wait_send()

    @pl.when(jnp.logical_not(wraps))
    def _():
        for c in kv[4:]:
            c.wait_send()

    for c in list(zrs.values()) + list(zls.values()) + list(z_legs.values()):
        c.wait_send()
    for n in range(NZ):
        for c in (*xsd[n], *xfd[n], *a_legs[n], *b_legs[n]):
            c.wait_send()
    for i in range(1, ND):
        f_legs[i].wait()

    @pl.when(swapped)
    def _():
        f_legs[0].wait()

    @pl.when(jnp.logical_not(swapped))
    def _():
        keep_own().wait()


def step(w, g, q, k, v, bias):
    dma = pltpu.SemaphoreType.DMA
    shape = jax.ShapeDtypeStruct
    hbm = [pl.BlockSpec(memory_space=pltpu.HBM)] * 5
    buf = pltpu.VMEM
    return pl.pallas_call(
        step_kernel,
        name="step",
        out_shape=(
            shape((TOK, WID), BF),
            shape((2, TOK, WID), BF),
            shape((TOK, WID), BF),
            shape((TOK, WID), F32),
            shape((TOK, WID), F32),
            shape((2, HEADS, TOK, HS), BF),
            shape((2, SUMC, WID), F32),
            shape((ND, ROWS, WID), BF),
        ),
        in_specs=hbm + vmem(1),
        out_specs=tuple(vmem(8)),
        scratch_shapes=[
            buf((NX, NZ, ROWS, WID), BF),
            buf((NH, TOK, WID), BF),
            buf((TOK, WID), BF),
            buf((TOK, WID), BF),
            buf((TOK, WID), BF),
            buf((TOK, WID), BF),
            buf((TOK, WID), BF),
            buf((NX, NZ, 2, SUMC, WID), BF),
            buf((TOK, WID), BF),
            buf((TOK, WID), BF),
            buf((HEADS, 3, TOK, TOK), F32),
            buf((WID, TOK), BF),
            buf((TOK, WID), BF),
            buf((NH, NZ, ROWS, WID), BF),
            buf((NH, TOK, WID), BF),
            buf((TOK, WID), F32),
            buf((TOK, WID), BF),
            buf((TOK, WID), BF),
            buf((TOK, WID), BF),
            buf((2, HEADS, TOK, HS), BF),
            buf((NX, NZ, 2, SUMC, WID), BF),
            buf((2, NZ, HALF, WID), BF),
            buf((2, NZ, ROWS, WID), BF),
            buf((2, NZ, ROWS, WID), BF),
            buf((NZ - 1, ROWS, WID), BF),
            buf((NZ - 1, ROWS, WID), BF),
            buf((ROWS, WID), BF),
            buf((NX - 1, NZ, 2, SUMC, WID), BF),
            buf((NZ, 2, SUMC, WID), BF),
            buf((NZ - 1, 2, SUMC, WID), BF),
            buf((TOK, WID), BF),
        ]
        + [dma((2,)), dma((7,))]
        + [dma((3,)), dma((3,)), dma((4,)), dma((4,))]
        + [dma((NZ,))] * 8
        + [dma((2, TOK // ROWS))] * 2
        + [dma((3,)), dma((3,))]
        + [dma((3,)), dma((3,)), dma((4,)), dma((4,)), dma((2, NX - 1)), dma((2, NX - 1))]
        + [dma((TOK // ROWS,))] * 3
        + [dma((2, NZ))] * 4
        + [dma((NZ - 1,)), dma((NZ - 1,)), dma((ND,)), dma((ND,)), dma]
        + [dma((2, HEADS)), dma((2, HEADS)), dma((3,)), dma((3,))]
        + [dma((NX - 1,)), dma((NX - 1,)), dma((NZ - 1,)), dma((NZ - 1,))],
        compiler_params=pltpu.CompilerParams(
            collective_id=0, has_side_effects=True, vmem_limit_bytes=36 << 20
        ),
    )(*(pltpu.with_memory_space_constraint(a, pltpu.HBM) for a in (w, g, q, k, v)), bias)


def finish_kernel(pown, pin, dq, dko, dvo, back, far, fin, proj, qg, kg, vg, wg):
    proj[...] = (pown[...].astype(F32) + pin[0].astype(F32) + pin[1].astype(F32)).astype(BF)
    qg[...] = dq[...]
    for j, (out, mine) in enumerate(((kg, dko), (vg, dvo))):
        for n in range(HEADS):
            cols = pl.ds(n * HS, HS)
            out[pl.ds(0, TOK - 16), cols] = (
                mine[pl.ds(0, TOK - 16), cols] + back[j, n, pl.ds(0, TOK - 16)].astype(F32)
            ).astype(BF)
            tail = mine[pl.ds(TOK - 16, 16), cols] + back[j, n, pl.ds(TOK - 16, 16)].astype(F32)
            tail += jnp.concatenate([jnp.zeros((SUMC, HS), F32), far[j, :, cols]], axis=0)
            out[pl.ds(TOK - 16, 16), cols] = tail.astype(BF)
    wg[...] = (fin[0].astype(F32) + fin[1].astype(F32)) + (fin[2].astype(F32) + fin[3].astype(F32))


def finish(*parts):
    return pl.pallas_call(
        finish_kernel,
        name="finish",
        out_shape=(jax.ShapeDtypeStruct((TOK, WID), BF),) * 4 + (jax.ShapeDtypeStruct((ROWS, WID), F32),),
        in_specs=vmem(8),
        compiler_params=pltpu.CompilerParams(vmem_limit_bytes=16 << 20),
    )(*parts)


def body(queries, key_rows, value_rows, out_weight, sum_lists, out_grad):
    q, k, v, g = queries[0], key_rows[0], value_rows[0], out_grad[0]
    strides = jnp.arange(FSDP, dtype=jnp.int32)
    block = lax.axis_index("fsdp") * 2 + jnp.arange(2, dtype=jnp.int32)
    named = jnp.any(sum_lists[0][:, :, None] == strides[None, None, :], axis=1)
    usable = named & ((strides[None, :] + 1) * STRIDE <= (block[:, None] - 2) * BLK)
    bias = jnp.where(usable, 0.0, NEG).astype(F32)
    bias = jnp.broadcast_to(bias.T[:, None, :, None], (FSDP, SUMC, 2, BLK)).reshape(TOK, TOK)
    proj, qg, kg, vg, wg = finish(*step(out_weight, g, q, k, v, bias))
    return proj[None], qg[None], kg[None], vg[None], wg


def solution(mesh):
    tokens = P("dp", "fsdp", "head")
    return jax.shard_map(
        body,
        mesh=mesh,
        in_specs=(tokens, tokens, tokens, P("fsdp", "head"), P("dp", "fsdp", None), tokens),
        out_specs=(tokens, tokens, tokens, tokens, P("fsdp", "head")),
        check_vma=False,
    )
```
